32 devices in a mesh: groups: 2 (over x), seq: 16 (over z, y, core).
Axes of the slice: x: 2, y: 2, z: 4, core: 2. Of those that a mesh axis runs over, the one named last changes fastest.
Arguments:
- tokens: bfloat16 [8192, 4096], P(('groups', 'seq')), parts along dimension 0, may hold values from -14 to 14, as said below
- norm_gain: float32 [4096], replicated, may hold values from 0.25 to 1.75
- w_query: bfloat16 [4096, 2048], P('seq'), may hold values from -1 to 1, as said below
- w_key: bfloat16 [4096, 512], P('seq'), may hold values from -24 to 24
- w_value: bfloat16 [4096, 512], P('seq'), may hold values from -0.09375 to 0.09375
- passage_blocks: int32 [64], P(('groups', 'seq')), parts along dimension 0, may hold values from 0 to 9, as said below
Outputs:
- attended: bfloat16 [8192, 2048], P(('groups', 'seq')), parts along dimension 0
The draws below stay inside these ranges and needn't reach their ends.
There are 2 independent parts, one for each index of `groups`. The reference program is written for one: setup_inputs(seed, part) draws one part's arguments, and reference() takes and returns one part's arrays. A program takes and returns all parts, laid end to end along the dimension named above; an argument that names none is the same for every part. Nothing has to cross between parts.
Inputs may be any that keep to these rules, and one draw needn't show every extreme that they name: `passage_blocks`: passage numbers never fall along the row; each passage covers 1 to 7 whole blocks; the first and the last passage of the row cover exactly 7. `tokens`: hidden states of order one. `w_query`: entries of order 4096 ** -0.5.
All inputs are finite; a program needn't handle non-finite values.
Results may differ from the reference program's by a relative error of at most 0.0049.
The reference program's roundings to bfloat16 on the way (of `normed`, `query` and `rounded`) count: a program that leaves them out, or rounds other values in their place, can miss the bound.
Values may be sent and summed in bfloat16 or wider, within the bound.
A program may use at most 128 MiB of HBM per device.

```python
import jax
import jax.numpy as jnp
from jax import lax

D = 4096
HD = 128
QH = 16
KVH = 4
BLOCK = 128
REACH = 3
TOK_DEV = 256
NBLK = 32
TOKENS = 4096
MOST_BLK = 7
PASSAGES = 10
N_SEQ = 16


def query_matrix(key):
    sample = jax.random.normal(jax.random.fold_in(key, 11), (D, QH * HD), jnp.float32)
    return jnp.clip(sample, -6.0, 6.0) * D ** (-0.5)


def draw_w_query(key, part):
    return query_matrix(key).astype(jnp.bfloat16)


def draw_w_key(key, part):
    jitter = jnp.clip(jax.random.normal(jax.random.fold_in(key, 12), (D, KVH * HD), jnp.float32), -6.0, 6.0) * D ** (-0.5)
    return jitter.astype(jnp.bfloat16)


def draw_tokens(key, part):
    sample = jax.random.normal(jax.random.fold_in(key, 23), (TOKENS, D), jnp.float32)
    return jnp.clip(sample, -6.0, 6.0).astype(jnp.bfloat16)


def draw_passage_blocks(key, part):
    middle_blocks = NBLK - 2 * MOST_BLK
    middle_count = PASSAGES - 2
    extra_total = middle_blocks - middle_count
    slots = middle_count * (MOST_BLK - 1)
    order = jax.random.permutation(jax.random.fold_in(key, 31), slots)
    owners = (order[:extra_total] // (MOST_BLK - 1)).astype(jnp.int32)
    labels = jnp.arange(middle_count, dtype=jnp.int32)
    extra = jnp.sum((owners[:, None] == labels[None, :]).astype(jnp.int32), axis=0)
    lengths = 1 + extra
    ends = jnp.cumsum(lengths).astype(jnp.int32)
    positions = jnp.arange(middle_blocks, dtype=jnp.int32)
    middle_ids = 1 + jnp.sum((positions[:, None] >= ends[None, :]).astype(jnp.int32), axis=1)
    head_ids = jnp.zeros((MOST_BLK,), jnp.int32)
    tail_ids = jnp.full((MOST_BLK,), PASSAGES - 1, jnp.int32)
    return jnp.concatenate([head_ids, middle_ids.astype(jnp.int32), tail_ids]).astype(jnp.int32)


def level_of(stream_key, extent, cuts, low, largest):
    gain = 1.0
    for position, parts in cuts:
        draws = jax.random.uniform(jax.random.fold_in(jax.random.fold_in(stream_key, 6), position), (parts,), jnp.float32, low / len(cuts), largest / len(cuts))
        gain = gain * jnp.repeat(jnp.exp(draws), extent[position] // parts).reshape((-1,) + (1,) * (len(extent) - 1 - position))
    return gain


def scatter_about(stream_key, shape, deviation, reach, shards=(), kind=jnp.bfloat16):
    drawn = jax.random.normal(stream_key, shape, jnp.float32) * deviation
    if len(shards) > 0:
        drawn = level_of(stream_key, shape, shards, -0.22, 0.18) * drawn
    return jnp.clip(drawn, min=-reach, max=reach).astype(kind)


def setup_inputs(seed: int = 0, part: int = 0) -> dict:
    key_of = jax.random.split(jax.random.key(seed), 7)
    own_keys = jax.random.split(jax.random.fold_in(key_of[6], part), 7)
    return {
        "tokens": draw_tokens(jax.random.fold_in(jax.random.fold_in(key_of[6], part), 71), part),
        "norm_gain": jnp.clip(1.0 + 0.15 * jax.random.normal(key_of[1], (D,), jnp.float32), 0.25, 1.75),
        "w_query": draw_w_query(jax.random.fold_in(key_of[6], 71), part),
        "w_key": draw_w_key(jax.random.fold_in(key_of[6], 71), part),
        "w_value": scatter_about(key_of[4], (D, KVH * HD), D ** -0.5, 0.09375, ((0, 16),)),
        "passage_blocks": draw_passage_blocks(jax.random.fold_in(jax.random.fold_in(key_of[6], part), 71), part),
    }


def normalize(tokens, norm_gain):
    widened = tokens.astype(jnp.float32)
    inverse = lax.rsqrt(lax.optimization_barrier(jnp.mean(widened * widened, axis=-1, keepdims=True)) + 1e-05)
    return (widened * inverse * norm_gain).astype(jnp.bfloat16)

def attend_window(query, keys, values, query_ids, key_ids):
    row_count = query.shape[0]
    key_count = keys.shape[0]
    group = QH // KVH
    query_heads = query.reshape(row_count, KVH, group, HD).transpose(1, 0, 2, 3)
    key_heads = keys.reshape(key_count, KVH, HD).transpose(1, 0, 2)
    value_heads = values.reshape(key_count, KVH, HD).transpose(1, 0, 2)
    allowed = query_ids[:, None] == key_ids[None, :]

    def one_head(operands):
        head_query, head_keys, head_values = operands
        scores = jnp.einsum('tgd,sd->gts', head_query.astype(jnp.float32), head_keys.astype(jnp.float32)) * HD ** (-0.5)
        scores = jnp.where(allowed[None], scores, -1e+30)
        row_max = lax.optimization_barrier(jnp.max(scores, axis=-1, keepdims=True))
        weights = jnp.exp(scores - row_max)
        row_total = lax.optimization_barrier(jnp.sum(weights, axis=-1, keepdims=True))
        rounded = lax.optimization_barrier(weights.astype(jnp.bfloat16))
        mixed = jnp.einsum('gts,sd->tgd', rounded.astype(jnp.float32), head_values.astype(jnp.float32))
        return mixed / row_total.transpose(1, 0, 2)
    stacked = lax.map(one_head, (query_heads, key_heads, value_heads))
    return stacked.transpose(1, 0, 2, 3).reshape(row_count, QH * HD)

def reference(tokens, norm_gain, w_query, w_key, w_value, passage_blocks):
    normed = normalize(tokens, norm_gain)
    query = jnp.dot(normed, w_query, preferred_element_type=jnp.float32).astype(jnp.bfloat16)
    keys = jnp.dot(normed, w_key, preferred_element_type=jnp.float32).astype(jnp.bfloat16)
    values = jnp.dot(normed, w_value, preferred_element_type=jnp.float32).astype(jnp.bfloat16)
    passage = jnp.repeat(passage_blocks + 1, BLOCK).astype(jnp.int32)
    margin = REACH * TOK_DEV
    keys_wide = jnp.pad(keys, ((margin, margin), (0, 0)))
    values_wide = jnp.pad(values, ((margin, margin), (0, 0)))
    passage_wide = jnp.pad(passage, (margin, margin))
    window_len = (2 * REACH + 1) * TOK_DEV

    def one_shard(index):
        first_row = (index * TOK_DEV).astype(jnp.int32)
        shard_query = lax.dynamic_slice_in_dim(query, first_row, TOK_DEV, 0)
        shard_ids = lax.dynamic_slice_in_dim(passage, first_row, TOK_DEV, 0)
        near_keys = lax.dynamic_slice_in_dim(keys_wide, first_row, window_len, 0)
        near_values = lax.dynamic_slice_in_dim(values_wide, first_row, window_len, 0)
        near_ids = lax.dynamic_slice_in_dim(passage_wide, first_row, window_len, 0)
        return attend_window(shard_query, near_keys, near_values, shard_ids, near_ids).astype(jnp.bfloat16)
    result = lax.map(one_shard, jnp.arange(N_SEQ, dtype=jnp.int32))
    return result.reshape(TOKENS, QH * HD)
```

```python
import functools
import math

import jax
import jax.numpy as jnp
from jax import lax
from jax.experimental import pallas as pl
from jax.experimental.pallas import tpu as pltpu
from jax.sharding import PartitionSpec as P

HD = 128
QH = 16
KVH = 4
REACH = 3
GQ = QH // KVH
MESH = pl.DeviceIdType.MESH
SETS = 2 + GQ
SW = 2 * HD
PIECES = 4
SLOTS = 2 * REACH + 4
NCH = 2


def kernel(n_chips, tok_ref, gain_ref, wq_ref, wk_ref, wv_ref, id_ref, out_ref,
           xraw, xn, wkv, wq0, wq1, qbuf, win, onehot, idwin, obuf,
           send_sem, loc_sem, init_sem, zsem, xsem, tok_sem, id_sem, halo_sem, out_sem):
    nz = n_chips // 2
    rows, width = tok_ref.shape
    g = lax.axis_index("groups")
    s = lax.axis_index("seq")
    gx = lax.rem(g, 2)
    gp = g + 1 - 2 * gx
    c = lax.rem(s, 2)
    p = s // 2
    y = lax.rem(p, 2)
    z = p // 2
    me4 = 2 * y + c
    sib4 = 2 * y + 1 - c
    ys4 = 2 * (1 - y) + c
    yo4 = 2 * (1 - y) + 1 - c

    sib = (g, 4 * z + sib4)
    ysame = (g, 4 * z + ys4)
    yother = (g, 4 * z + yo4)
    twin = (gp, s)
    zm, zp = (g, s - 4), (g, s + 4)
    has_zm, has_zp = z >= 1, z + 1 < nz

    sends = []
    counter = [0]

    def guarded(cond, f):
        if cond is None:
            f()
        else:
            pl.when(cond)(f)

    def send(src, dst, rsem, dev, cond=None):
        d = pltpu.make_async_remote_copy(src_ref=src, dst_ref=dst, send_sem=send_sem.at[counter[0]],
                                         recv_sem=rsem, device_id=dev, device_id_type=MESH)
        counter[0] += 1
        guarded(cond, d.start)
        sends.append((cond, d))

    def recv(dst, rsem, dev, cond=None):
        d = pltpu.make_async_remote_copy(src_ref=dst, dst_ref=dst, send_sem=send_sem.at[0],
                                         recv_sem=rsem, device_id=dev, device_id_type=MESH)
        guarded(cond, d.wait_recv)

    def local(src, dst, i):
        d = pltpu.make_async_copy(src, dst, loc_sem.at[i])
        d.start()
        return d

    bufs = (wkv, wq0, wq1)

    def columns(head, i):
        return pl.ds(pl.multiple_of(head * HD if i < 2 else head * (GQ * HD) + (i - 2) * HD, HD), HD)

    weights = (wk_ref, wv_ref) + (wq_ref,) * GQ
    places = tuple((bufs[i // 2], slice(i % 2 * HD, i % 2 * HD + HD)) for i in range(SETS))

    def unit(t, zz, half):
        buf, lanes = places[t]
        return buf.at[zz, :, :, half, :, lanes]

    def mates(t, half):
        buf, lanes = places[t]
        return buf.at[z, 1 - y, :, half, :, lanes]

    def full_part(i, head, yy, cc):
        buf, lanes = places[i]
        return weights[i].at[:, :, columns(head, i)], buf.at[z, yy, cc, :, :, lanes]

    def half_part(i, head, yy, cc):
        buf, lanes = places[i]
        return weights[i].at[gx, :, columns(head, i)], buf.at[z, yy, cc, gx, :, lanes]

    loc_x = local(tok_ref, xraw.at[me4], SETS)
    loc_w = [local(*full_part(i, me4, y, c), i) for i in range(SETS)]

    barrier = pltpu.get_barrier_semaphore()
    for dev in (sib, ysame, yother, twin):
        pl.semaphore_signal(barrier, inc=1, device_id=dev, device_id_type=MESH)
    for cond, dev in ((has_zm, zm), (has_zp, zp)):
        guarded(cond, functools.partial(pl.semaphore_signal, barrier, inc=1, device_id=dev, device_id_type=MESH))

    first = lax.broadcasted_iota(jnp.int32, idwin.shape[1:], 0) == 0
    idwin[REACH + me4] = jnp.where(first, id_ref[0], id_ref[1]) + 1
    pl.semaphore_wait(barrier, 4 + jnp.where(has_zm, 1, 0) + jnp.where(has_zp, 1, 0))

    prow = rows // PIECES
    for i in range(SETS):
        for k, (dev, head) in enumerate(((ysame, ys4), (yother, yo4))):
            a, b = half_part(i, head, y, c)
            send(a, b, init_sem.at[i, 1 + k], dev)
        a, b = full_part(i, sib4, y, c)
        send(a, b, init_sem.at[i, 0], sib)
    for i, dev in enumerate((sib, ysame, yother)):
        own = idwin.at[REACH + me4]
        send(own, own, id_sem.at[i], dev)
    for j in range(PIECES):
        r = slice(j * prow, (j + 1) * prow)
        send(tok_ref.at[r], xraw.at[me4, r], tok_sem.at[0, j], ysame)
    send(tok_ref, xraw.at[me4], tok_sem.at[2, 0], sib)

    def blank(lo):
        def f():
            win[lo:lo + REACH] = jnp.zeros((REACH, rows, SW), jnp.bfloat16)
            idwin[lo:lo + REACH] = jnp.zeros((REACH,) + idwin.shape[1:], jnp.int32)
        return f

    def relay(t, d):
        if d == 0:
            loc_w[t].wait()
            recv(full_part(t, me4, y, 1 - c)[1], init_sem.at[t, 0], sib)
            recv(half_part(t, me4, 1 - y, c)[1], init_sem.at[t, 1], ysame)
            recv(half_part(t, me4, 1 - y, 1 - c)[1], init_sem.at[t, 2], yother)
            own = unit(t, z, gx)
            send(own, own, zsem.at[t, 1, 1], zm, has_zm)
            send(own, own, zsem.at[t, 0, 1], zp, has_zp)
            send(mates(t, gx), mates(t, gx), xsem.at[t, 0, 0], twin)
            return
        left, right = unit(t, z - d, gx), unit(t, z + d, gx)
        has_l, has_r = z >= d, z + d < nz
        recv(right, zsem.at[t, 1, d], zp, has_r)
        if d + 1 < nz:
            send(right, right, zsem.at[t, 1, d + 1], zm, has_r & has_zm)
        send(right, right, xsem.at[t, 1, d], twin, has_r)
        recv(left, zsem.at[t, 0, d], zm, has_l)
        if d + 1 < nz:
            send(left, left, zsem.at[t, 0, d + 1], zp, has_l & has_zp)
        send(left, left, xsem.at[t, 0, d], twin, has_l)

    def finish(pair):
        for t in (2 * pair, 2 * pair + 1):
            recv(mates(t, 1 - gx), xsem.at[t, 0, 0], twin)
            for d in range(1, nz):
                recv(unit(t, z + d, 1 - gx), xsem.at[t, 1, d], twin, z + d < nz)
                recv(unit(t, z - d, 1 - gx), xsem.at[t, 0, d], twin, z >= d)

    def normalize(slot, first=0, count=None):
        step = 16
        count = rows if count is None else count

        def body(i, _):
            r = pl.ds(pl.multiple_of(first + i * step, step), step)
            wide = xraw[slot, r, :].astype(jnp.float32)
            inv = lax.rsqrt(jnp.mean(wide * wide, axis=-1, keepdims=True) + 1e-05)
            xn[slot, r, :] = (wide * inv * gain_ref[...]).astype(jnp.bfloat16)
            return 0

        lax.fori_loop(0, count // step, body, 0)

    def tokens(j):
        r = slice(j * prow, (j + 1) * prow)
        recv(xraw.at[ys4, r], tok_sem.at[0, j], ysame)
        send(xraw.at[ys4, r], xraw.at[ys4, r], tok_sem.at[1, j], sib)
        normalize(ys4, j * prow, prow)
        recv(xraw.at[yo4, r], tok_sem.at[1, j], sib)
        normalize(yo4, j * prow, prow)

    def project(t, yy, ch):
        a = xn[pl.ds(2 * yy, 2), ch * HD:(ch + 1) * HD, :].reshape(2 * HD, width)
        r = jnp.dot(a, bufs[t][...].reshape(width, SW), preferred_element_type=jnp.float32).astype(jnp.bfloat16)
        for i in range(2):
            part = r[i * HD:(i + 1) * HD]
            if t == 0:
                win[REACH + 2 * yy + i, ch * HD:(ch + 1) * HD, :] = part
            else:
                for h in range(2):
                    qbuf[t - 1, 2 * yy + i, ch, h] = part[:, h * HD:(h + 1) * HD]

    def halo_send(yy, ch):
        r = slice(ch * HD, (ch + 1) * HD)
        for slot in range(4):
            mine = (slot // 2) == yy
            a = win.at[REACH + slot, r]
            if slot > 0:
                send(a, win.at[slot - 1, r], halo_sem.at[0, slot - 1, ch], zp, mine & has_zp)
            if slot < 3:
                send(a, win.at[REACH + 4 + slot, r], halo_sem.at[1, slot, ch], zm, mine & has_zm)

    def halo_recv():
        for j in range(REACH):
            for ch in range(NCH):
                r = slice(ch * HD, (ch + 1) * HD)
                recv(win.at[j, r], halo_sem.at[0, j, ch], zm, has_zm)
                recv(win.at[REACH + 4 + j, r], halo_sem.at[1, j, ch], zp, has_zp)

    def ids_send():
        for i, (slot, dev) in enumerate(((sib4, sib), (ys4, ysame), (yo4, yother))):
            recv(idwin.at[REACH + slot], id_sem.at[i], dev)
        send(idwin.at[4:7], idwin.at[0:3], id_sem.at[3], zp, has_zp)
        send(idwin.at[3:6], idwin.at[7:10], id_sem.at[4], zm, has_zm)

    def ids_recv():
        recv(idwin.at[0:3], id_sem.at[3], zm, has_zm)
        recv(idwin.at[7:10], id_sem.at[4], zp, has_zp)

    rate = HD ** (-0.5) * math.log2(math.e)
    span = (2 * REACH + 1) * NCH - 1

    def fill_onehot():
        def body(i, _):
            lane = lax.broadcasted_iota(jnp.int32, (HD, HD), 1)
            onehot[i] = jnp.where(lane == i, 1.0, 0.0).astype(jnp.bfloat16)
            return 0
        lax.fori_loop(0, SLOTS * NCH, body, 0)

    def attend(slot, t):
        lane = lax.broadcasted_iota(jnp.int32, (1, HD), 1)
        ids = jnp.zeros((1, HD), jnp.int32)
        for j in range(SLOTS * NCH):
            ids = jnp.where(lane == j, idwin[j // NCH, j % NCH:j % NCH + 1, :], ids)

        def body(qb, _):
            mine = idwin[REACH + slot, pl.ds(qb, 1), :]
            bias = jnp.where(ids == mine, 0.0, -1e30)
            bias = jnp.broadcast_to(bias, (2 * HD, HD)).astype(jnp.bfloat16)
            q = jnp.concatenate([qbuf[t, slot, qb].reshape(2 * HD, HD), bias], axis=1)
            at = pl.ds(NCH * slot + qb, span)
            kv = win.reshape(SLOTS * NCH, HD, SW)
            k = jnp.concatenate([kv[at, :, 0:HD].reshape(span * HD, HD),
                                 onehot[at].reshape(span * HD, HD)], axis=1)
            v = jnp.concatenate([kv[at, :, HD:SW].reshape(span * HD, HD),
                                 jnp.ones((span * HD, HD), jnp.bfloat16)], axis=1)
            sc = lax.dot_general(q, k, (((1,), (1,)), ((), ())), preferred_element_type=jnp.float32)
            top = jnp.max(sc, axis=-1, keepdims=True)
            w = jnp.exp2((sc - top) * rate).astype(jnp.bfloat16)
            o = jnp.dot(w, v, preferred_element_type=jnp.float32)
            o = (o[:, 0:HD] / o[:, HD:SW]).astype(jnp.bfloat16)
            rr = pl.ds(pl.multiple_of(qb * HD, HD), HD)
            obuf[t, slot, rr, 0:HD] = o[0:HD]
            obuf[t, slot, rr, HD:SW] = o[HD:SW]
            return 0

        lax.fori_loop(0, NCH, body, 0)

    def out_cols(head, t):
        return out_ref.at[:, pl.ds(pl.multiple_of(head * (GQ * HD) + t * SW, HD), SW)]

    out_local = []

    def attend_slots(t, group):
        for i, slot, dev in group:
            attend(slot, t)
            src = obuf.at[t, slot]
            if dev is None:
                out_local.append(local(src, out_cols(me4, t), SETS + 1 + t))
            else:
                send(src, out_cols(me4, t), out_sem.at[t, i], dev)

    order = sorted(((t, d) for t in range(SETS) for d in range(nz)),
                   key=lambda td: (nz - 1) * td[0] + (nz - 0.5) * td[1])
    after = {}

    def at_task(index, f):
        after.setdefault(min(index, len(order) - 1), []).append(f)

    def kv_early():
        finish(0)
        project(0, y, 0)
        project(0, y, 1)
        project(0, 1 - y, 0)

    def q_early():
        finish(1)
        project(1, y, 0)
        project(1, y, 1)
        project(1, 1 - y, 0)

    def own_tokens():
        loc_x.wait()
        normalize(me4)

    def sib_tokens():
        recv(xraw.at[sib4], tok_sem.at[2, 0], sib)
        normalize(sib4)
        fill_onehot()
        pl.when(z < 1)(blank(0))
        pl.when(z + 1 >= nz)(blank(REACH + 4))

    last = nz - 1
    at_task(order.index((2, 0)), own_tokens)
    at_task(order.index((3, 0)), ids_send)
    at_task(order.index((3, 0)), sib_tokens)
    at_task(order.index((0, last)), lambda: tokens(0))
    at_task(order.index((4, 1)), lambda: tokens(1))
    at_task(order.index((1, last)) + 2, kv_early)
    at_task(order.index((4, min(2, last))), lambda: tokens(2))
    at_task(order.index((3, last)) + 2, q_early)
    for i, (t, d) in enumerate(order):
        relay(t, d)
        for f in after.get(i, ()):
            f()
    halo_send(y, 0)
    halo_send(y, 1)
    halo_send(1 - y, 0)
    tokens(3)
    project(0, 1 - y, 1)
    halo_send(1 - y, 1)
    project(1, 1 - y, 1)
    finish(2)
    for yy in (1 - y, y):
        for ch in range(NCH):
            project(2, yy, ch)
    ids_recv()
    halo_recv()
    far = ((0, yo4, yother), (1, ys4, ysame))
    near = ((2, sib4, sib), (3, me4, None))
    attend_slots(0, far)
    attend_slots(1, far)
    attend_slots(0, near)
    attend_slots(1, near)
    for t in range(2):
        for i, (dev, head) in enumerate(((yother, yo4), (ysame, ys4), (sib, sib4))):
            recv(out_cols(head, t), out_sem.at[t, i], dev)
    for d in out_local:
        d.wait()
    for cond, d in sends:
        guarded(cond, d.wait_send)


def solution(mesh):
    n_seq = mesh.shape["seq"]
    n_chips = n_seq // 2
    nz = n_chips // 2

    def on_device(tokens, norm_gain, w_query, w_key, w_value, passage_blocks):
        rows, width = tokens.shape
        anywhere = pl.BlockSpec(memory_space=pl.ANY)
        vmem = pl.BlockSpec(memory_space=pltpu.VMEM)
        smem = pl.BlockSpec(memory_space=pltpu.SMEM)
        n_send = SETS * (4 * nz + 3) + 3 + 2 * PIECES + 1 + 2 + 12 * NCH + 6
        bf = jnp.bfloat16
        dma = pltpu.SemaphoreType.DMA
        half = w_query.shape[0] // 2
        weight = pltpu.VMEM((nz, 2, 2, 2, half, SW), bf)
        halves = [w.reshape(2, half, w.shape[1]) for w in (w_query, w_key, w_value)]
        return pl.pallas_call(
            functools.partial(kernel, n_chips),
            out_shape=jax.ShapeDtypeStruct((rows, QH * HD), bf),
            in_specs=[anywhere, vmem, anywhere, anywhere, anywhere, smem],
            out_specs=anywhere,
            scratch_shapes=[
                pltpu.VMEM((4, rows, width), bf),
                pltpu.VMEM((4, rows, width), bf),
                weight, weight, weight,
                pltpu.VMEM((2, 4, NCH, 2, HD, HD), bf),
                pltpu.VMEM((SLOTS, rows, SW), bf),
                pltpu.VMEM((SLOTS * NCH, HD, HD), bf),
                pltpu.VMEM((SLOTS, 8, HD), jnp.int32),
                pltpu.VMEM((2, 4, rows, SW), bf),
                dma((n_send,)), dma((SETS + 4,)), dma((SETS, 3)), dma((SETS, 2, nz)), dma((SETS, 2, nz)),
                dma((3, PIECES)), dma((5,)), dma((2, REACH, NCH)), dma((2, 3)),
            ],
            compiler_params=pltpu.CompilerParams(
                collective_id=0, has_side_effects=True, vmem_limit_bytes=60 * 2**20),
        )(tokens, norm_gain[None, :], *halves, passage_blocks)

    in_specs = (
        P(("groups", "seq"), None),
        P(),
        P("seq", None),
        P("seq", None),
        P("seq", None),
        P(("groups", "seq")),
    )
    out_specs = P(("groups", "seq"), None)
    return jax.shard_map(on_device, mesh=mesh, in_specs=in_specs, out_specs=out_specs, check_vma=False)
```

```python
import functools
import math

import jax
import jax.numpy as jnp
from jax import lax
from jax.experimental import pallas as pl
from jax.experimental.pallas import tpu as pltpu
from jax.sharding import PartitionSpec as P

HD = 128
QH = 16
KVH = 4
REACH = 3
GQ = QH // KVH
MESH = pl.DeviceIdType.MESH
SETS = 2 + GQ
SW = 2 * HD
PIECES = 8
SLOTS = 2 * REACH + 4
NCH = 2


def kernel(n_chips, tok_ref, gain_ref, wq_ref, wk_ref, wv_ref, id_ref, out_ref,
           gain, ids_in, starts, xraw, xn, wk_in, wv_in, wq_in, wbuf, qbuf, win, idwin, obuf,
           send_sem, loc_sem, init_sem, zsem, xsem, tok_sem, id_sem, halo_sem, out_sem):
    nz = n_chips // 2
    rows, width = tok_ref.shape
    g = lax.axis_index("groups")
    s = lax.axis_index("seq")
    gx = lax.rem(g, 2)
    gp = g + 1 - 2 * gx
    c = lax.rem(s, 2)
    p = s // 2
    y = lax.rem(p, 2)
    z = p // 2
    me4 = 2 * y + c
    sib4 = 2 * y + 1 - c
    ys4 = 2 * (1 - y) + c
    yo4 = 2 * (1 - y) + 1 - c

    sib = (g, 4 * z + sib4)
    ysame = (g, 4 * z + ys4)
    yother = (g, 4 * z + yo4)
    twin = (gp, s)
    zm, zp = (g, s - 4), (g, s + 4)
    has_zm, has_zp = z >= 1, z + 1 < nz

    sends = []
    counter = [0]

    def guarded(cond, f):
        if cond is None:
            f()
        else:
            pl.when(cond)(f)

    def send(src, dst, rsem, dev, cond=None):
        d = pltpu.make_async_remote_copy(src_ref=src, dst_ref=dst, send_sem=send_sem.at[counter[0]],
                                         recv_sem=rsem, device_id=dev, device_id_type=MESH)
        counter[0] += 1
        guarded(cond, d.start)
        sends.append((cond, d))

    def recv(dst, rsem, dev, cond=None):
        d = pltpu.make_async_remote_copy(src_ref=dst, dst_ref=dst, send_sem=send_sem.at[0],
                                         recv_sem=rsem, device_id=dev, device_id_type=MESH)
        guarded(cond, d.wait_recv)

    def local(src, dst, i):
        d = pltpu.make_async_copy(src, dst, loc_sem.at[i])
        d.start()
        return d

    def columns(head, i):
        return pl.ds(pl.multiple_of(head * HD if i < 2 else head * (GQ * HD) + (i - 2) * HD, HD), HD)

    weights = (wk_in, wv_in) + (wq_in,) * GQ

    def unit(t, zz, half):
        return wbuf.at[t, half, zz]

    def mates(t, half):
        return wbuf.at[t, half, z, 1 - y]

    def full_part(i, head, yy, cc):
        return weights[i].at[:, :, columns(head, i)], wbuf.at[i, :, z, yy, cc]

    def half_part(i, head, yy, cc):
        return weights[i].at[gx, :, columns(head, i)], wbuf.at[i, gx, z, yy, cc]

    loc_in = [local(src, dst, SETS + 3 + i)
              for i, (src, dst) in enumerate(((wk_ref, wk_in), (wv_ref, wv_in), (wq_ref, wq_in),
                                              (id_ref, ids_in), (gain_ref, gain)))]

    barrier = pltpu.get_barrier_semaphore()
    for dev in (sib, ysame, yother, twin):
        pl.semaphore_signal(barrier, inc=1, device_id=dev, device_id_type=MESH)
    for cond, dev in ((has_zm, zm), (has_zp, zp)):
        guarded(cond, functools.partial(pl.semaphore_signal, barrier, inc=1, device_id=dev, device_id_type=MESH))

    loc_in[3].wait()
    for i in range(NCH):
        idwin[NCH * (REACH + me4) + i] = jnp.full(idwin.shape[1:], ids_in[i] + 1, jnp.int32)
    pl.semaphore_wait(barrier, 4 + jnp.where(has_zm, 1, 0) + jnp.where(has_zp, 1, 0))

    prow = rows // PIECES
    for i in range(SETS):
        if i < 3:
            loc_in[i].wait()
        for k, (dev, head) in enumerate(((ysame, ys4), (yother, yo4))):
            a, b = half_part(i, head, y, c)
            send(a, b, init_sem.at[i, 1 + k], dev)
        a, b = full_part(i, sib4, y, c)
        send(a, b, init_sem.at[i, 0], sib)
    loc_w = [local(*full_part(i, me4, y, c), i) for i in range(SETS)]
    loc_x = local(tok_ref, xraw.at[me4], SETS)
    for i, dev in enumerate((sib, ysame, yother)):
        own = idwin.at[pl.ds(NCH * (REACH + me4), NCH)]
        send(own, own, id_sem.at[i], dev)
    for j in range(PIECES):
        r = slice(j * prow, (j + 1) * prow)
        send(tok_ref.at[r], xraw.at[me4, r], tok_sem.at[0, j], ysame)
    send(tok_ref, xraw.at[me4], tok_sem.at[2, 0], sib)

    def blank(lo):
        def f():
            win[lo:lo + REACH] = jnp.zeros((REACH, rows, SW), jnp.bfloat16)
            idwin[NCH * lo:NCH * (lo + REACH)] = jnp.zeros((NCH * REACH,) + idwin.shape[1:], jnp.int32)
        return f

    def pieces(t):
        return 2 if t == 0 else 1

    def part(t, zz, half, k):
        ref = unit(t, zz, half)
        return ref if pieces(t) == 1 else ref.at[lax.rem(y + k, 2)]

    def gather(t):
        loc_w[t].wait()
        recv(full_part(t, me4, y, 1 - c)[1], init_sem.at[t, 0], sib)
        if pieces(t) == 2:
            relay_part(t, 0, 0)
        recv(half_part(t, me4, 1 - y, c)[1], init_sem.at[t, 1], ysame)
        recv(half_part(t, me4, 1 - y, 1 - c)[1], init_sem.at[t, 2], yother)
        send(mates(t, gx), mates(t, gx), xsem.at[t, 0, 0], twin)

    def relay_part(t, d, k):
        left, right = part(t, z - d, gx, k), part(t, z + d, gx, k)
        has_l, has_r = z >= d, z + d < nz
        if d == 0:
            send(left, left, zsem.at[t, 1, 1, k], zm, has_zm)
            send(left, left, zsem.at[t, 0, 1, k], zp, has_zp)
            return
        recv(right, zsem.at[t, 1, d, k], zp, has_r)
        if d + 1 < nz:
            send(right, right, zsem.at[t, 1, d + 1, k], zm, has_r & has_zm)
        recv(left, zsem.at[t, 0, d, k], zm, has_l)
        if d + 1 < nz:
            send(left, left, zsem.at[t, 0, d + 1, k], zp, has_l & has_zp)

    def relay(t, d):
        for k in range(pieces(t)):
            if d > 0 or k > 0 or pieces(t) == 1:
                relay_part(t, d, k)
        if d > 0:
            left, right = unit(t, z - d, gx), unit(t, z + d, gx)
            send(right, right, xsem.at[t, 1, d], twin, z + d < nz)
            send(left, left, xsem.at[t, 0, d], twin, z >= d)

    def finish(pair):
        for t in (2 * pair, 2 * pair + 1):
            recv(mates(t, 1 - gx), xsem.at[t, 0, 0], twin)
            for d in range(1, nz):
                recv(unit(t, z + d, 1 - gx), xsem.at[t, 1, d], twin, z + d < nz)
                recv(unit(t, z - d, 1 - gx), xsem.at[t, 0, d], twin, z >= d)

    def normalize(slot, first=0, count=None):
        step = 16
        count = rows if count is None else count

        def body(i, _):
            r = pl.ds(pl.multiple_of(first + i * step, step), step)
            wide = xraw[slot, r, :].astype(jnp.float32)
            inv = lax.rsqrt(jnp.mean(wide * wide, axis=-1, keepdims=True) + 1e-05)
            xn[slot, r, :] = (wide * inv * gain[...]).astype(jnp.bfloat16)
            return 0

        lax.fori_loop(0, count // step, body, 0)

    def tokens(start, stop):
        for j in range(start, stop):
            r = slice(j * prow, (j + 1) * prow)
            recv(xraw.at[ys4, r], tok_sem.at[0, j], ysame)
            send(xraw.at[ys4, r], xraw.at[ys4, r], tok_sem.at[1, j], sib)
            normalize(ys4, j * prow, prow)
        for j in range(start, stop):
            recv(xraw.at[yo4, j * prow:(j + 1) * prow], tok_sem.at[1, j], sib)
            normalize(yo4, j * prow, prow)

    def project(t, yy, ch):
        a = xn[pl.ds(2 * yy, 2), ch * HD:(ch + 1) * HD, :].reshape(2 * HD, width)
        w = jnp.concatenate(
            [jnp.concatenate([wbuf[2 * t + i, h, zz, yc // 2, yc % 2] for i in range(2)], axis=1)
             for zz in range(nz) for yc in range(4) for h in range(2)], axis=0)
        r = jnp.dot(a, w, preferred_element_type=jnp.float32).astype(jnp.bfloat16)
        for i in range(2):
            part = r[i * HD:(i + 1) * HD]
            if t == 0:
                win[REACH + 2 * yy + i, ch * HD:(ch + 1) * HD, :] = part
            else:
                for h in range(2):
                    qbuf[t - 1, 2 * yy + i, ch, h] = part[:, h * HD:(h + 1) * HD]

    def halo_send(yy, ch):
        r = slice(ch * HD, (ch + 1) * HD)
        for slot in range(4):
            mine = (slot // 2) == yy
            a = win.at[REACH + slot, r]
            if slot > 0:
                send(a, win.at[slot - 1, r], halo_sem.at[0, slot - 1, ch], zp, mine & has_zp)
            if slot < 3:
                send(a, win.at[REACH + 4 + slot, r], halo_sem.at[1, slot, ch], zm, mine & has_zm)

    def halo_recv():
        for j in range(REACH):
            for ch in range(NCH):
                r = slice(ch * HD, (ch + 1) * HD)
                recv(win.at[j, r], halo_sem.at[0, j, ch], zm, has_zm)
                recv(win.at[REACH + 4 + j, r], halo_sem.at[1, j, ch], zp, has_zp)

    def ids_send():
        for i, (slot, dev) in enumerate(((sib4, sib), (ys4, ysame), (yo4, yother))):
            recv(idwin.at[pl.ds(NCH * (REACH + slot), NCH)], id_sem.at[i], dev)
        edge = NCH * REACH
        a = NCH * (REACH + 4)
        send(idwin.at[a - edge:a], idwin.at[0:edge], id_sem.at[3], zp, has_zp)
        send(idwin.at[edge:2 * edge], idwin.at[a:a + edge], id_sem.at[4], zm, has_zm)

    def ids_recv():
        edge = NCH * REACH
        a = NCH * (REACH + 4)
        recv(idwin.at[0:edge], id_sem.at[3], zm, has_zm)
        recv(idwin.at[a:a + edge], id_sem.at[4], zp, has_zp)
        lane = lax.broadcasted_iota(jnp.int32, (8, HD), 1)
        ids = jnp.zeros((8, HD), jnp.int32)
        for j in range(SLOTS * NCH):
            ids = jnp.where(lane == j, idwin[j], ids)
        for j in range(edge, a):
            opening = jnp.min(jnp.where(ids == idwin[j], lane, j))
            starts[j - edge] = jnp.maximum(opening, j - edge)

    rate = HD ** (-0.5) * math.log2(math.e)
    span = REACH * NCH + 1

    def attend(slot, t):
        kv = win.reshape(SLOTS * NCH, HD, SW)
        for qb in range(NCH):
            mine = idwin[NCH * (REACH + slot) + qb, 0:1, :]
            start = starts[NCH * slot + qb]
            bias = jnp.concatenate(
                [jnp.where(idwin[start + j, 0:1, :] == mine, 0.0, -1e30) for j in range(span)], axis=1)
            q = qbuf[t, slot, qb].reshape(2 * HD, HD)
            at = pl.ds(start, span)
            k = kv[at, :, 0:HD].reshape(span * HD, HD)
            v = jnp.concatenate([kv[at, :, HD:SW].reshape(span * HD, HD),
                                 jnp.ones((span * HD, HD), jnp.bfloat16)], axis=1)
            sc = lax.dot_general(q, k, (((1,), (1,)), ((), ())), preferred_element_type=jnp.float32) + bias
            top = jnp.max(sc, axis=-1, keepdims=True)
            w = jnp.exp2((sc - top) * rate).astype(jnp.bfloat16)
            o = jnp.dot(w, v, preferred_element_type=jnp.float32)
            o = (o[:, 0:HD] / o[:, HD:SW]).astype(jnp.bfloat16)
            rr = slice(qb * HD, (qb + 1) * HD)
            obuf[t, slot, rr, 0:HD] = o[0:HD]
            obuf[t, slot, rr, HD:SW] = o[HD:SW]

    def out_cols(head, t):
        return out_ref.at[:, pl.ds(pl.multiple_of(head * (GQ * HD) + t * SW, HD), SW)]

    out_local = []

    def attend_slots(t, group):
        for i, slot, dev in group:
            attend(slot, t)
            src = obuf.at[t, slot]
            if dev is None:
                out_local.append(local(src, out_cols(me4, t), SETS + 1 + t))
            else:
                send(src, out_cols(me4, t), out_sem.at[t, i], dev)

    order = sorted(((t, d) for t in range(SETS) for d in range(nz)),
                   key=lambda td: (nz - 1) * td[0] + (nz - 0.5) * td[1])
    after = {}

    def at_task(index, f):
        after.setdefault(min(index, len(order) - 1), []).append(f)

    def kv_early():
        finish(0)
        project(0, y, 0)
        project(0, y, 1)
        halo_send(y, 0)
        halo_send(y, 1)
        project(0, 1 - y, 0)
        halo_send(1 - y, 0)

    def own_tokens():
        loc_x.wait()
        loc_in[4].wait()
        normalize(me4)

    def sib_tokens():
        recv(xraw.at[sib4], tok_sem.at[2, 0], sib)
        normalize(sib4)
        pl.when(z < 1)(blank(0))
        pl.when(z + 1 >= nz)(blank(REACH + 4))

    last = nz - 1
    at_task(order.index((2, 0)), own_tokens)
    at_task(order.index((3, 0)), ids_send)
    at_task(order.index((3, 0)), sib_tokens)
    at_task(order.index((0, last)), lambda: tokens(0, 2))
    at_task(order.index((4, 1)), lambda: tokens(2, 4))
    at_task(order.index((1, last)) + 2, kv_early)
    at_task(order.index((4, min(2, last))), lambda: tokens(4, 6))
    at_task(len(order) - 3, lambda: tokens(6, 7))
    gathered = 0
    for i, (t, d) in enumerate(order[:-1]):
        while gathered < SETS and (gathered <= t or d > 0 or gathered <= i + 1):
            gather(gathered)
            gathered += 1
        relay(t, d)
        for f in after.get(i, ()):
            f()
    tokens(7, 8)
    project(0, 1 - y, 1)
    halo_send(1 - y, 1)
    finish(1)
    project(1, 1 - y, 0)
    project(1, 1 - y, 1)
    relay(*order[-1])
    project(1, y, 0)
    project(1, y, 1)
    ids_recv()
    halo_recv()
    far = ((0, yo4, yother), (1, ys4, ysame))
    near = ((2, sib4, sib), (3, me4, None))
    attend_slots(0, far)
    attend_slots(0, near)
    finish(2)
    for yy in (1 - y, y):
        for ch in range(NCH):
            project(2, yy, ch)
    attend_slots(1, far)
    attend_slots(1, near)
    for t in range(2):
        for i, (dev, head) in enumerate(((yother, yo4), (ysame, ys4), (sib, sib4))):
            recv(out_cols(head, t), out_sem.at[t, i], dev)
    for d in out_local:
        d.wait()
    for cond, d in sends:
        guarded(cond, d.wait_send)


def solution(mesh):
    n_seq = mesh.shape["seq"]
    n_chips = n_seq // 2
    nz = n_chips // 2

    def on_device(tokens, norm_gain, w_query, w_key, w_value, passage_blocks):
        rows, width = tokens.shape
        anywhere = pl.BlockSpec(memory_space=pl.ANY)
        hbm = pl.BlockSpec(memory_space=pltpu.HBM)
        n_send = SETS * (4 * nz + 3) + 2 * nz + 3 + 2 * PIECES + 1 + 2 + 12 * NCH + 6
        bf = jnp.bfloat16
        dma = pltpu.SemaphoreType.DMA
        half = w_query.shape[0] // 2
        halves = [w.reshape(2, half, w.shape[1]) for w in (w_query, w_key, w_value)]
        return pl.pallas_call(
            functools.partial(kernel, n_chips),
            out_shape=jax.ShapeDtypeStruct((rows, QH * HD), bf),
            in_specs=[hbm] * 6,
            out_specs=anywhere,
            scratch_shapes=[
                pltpu.VMEM((1, width), jnp.float32),
                pltpu.SMEM(passage_blocks.shape, jnp.int32),
                pltpu.SMEM((4 * NCH,), jnp.int32),
                pltpu.VMEM((4, rows, width), bf),
                pltpu.VMEM((4, rows, width), bf),
                *(pltpu.VMEM((2, half, w.shape[1]), bf) for w in (w_key, w_value, w_query)),
                pltpu.VMEM((SETS, 2, nz, 2, 2, half, HD), bf),
                pltpu.VMEM((2, 4, NCH, 2, HD, HD), bf),
                pltpu.VMEM((SLOTS, rows, SW), bf),
                pltpu.VMEM((SLOTS * NCH, 8, HD), jnp.int32),
                pltpu.VMEM((2, 4, rows, SW), bf),
                dma((n_send,)), dma((SETS + 8,)), dma((SETS, 3)), dma((SETS, 2, nz, 2)), dma((SETS, 2, nz)),
                dma((3, PIECES)), dma((5,)), dma((2, REACH, NCH)), dma((2, 3)),
            ],
            compiler_params=pltpu.CompilerParams(
                collective_id=0, has_side_effects=True, vmem_limit_bytes=52 * 2**20),
        )(*(pltpu.with_memory_space_constraint(a, pltpu.HBM)
            for a in (tokens, norm_gain[None, :], *halves, passage_blocks)))

    in_specs = (
        P(("groups", "seq"), None),
        P(),
        P("seq", None),
        P("seq", None),
        P("seq", None),
        P(("groups", "seq")),
    )
    out_specs = P(("groups", "seq"), None)
    return jax.shard_map(on_device, mesh=mesh, in_specs=in_specs, out_specs=out_specs, check_vma=False)
```

```python
import functools
import math

import jax
import jax.numpy as jnp
from jax import lax
from jax.experimental import pallas as pl
from jax.experimental.pallas import tpu as pltpu
from jax.sharding import PartitionSpec as P

HD = 128
QH = 16
KVH = 4
REACH = 3
GQ = QH // KVH
MESH = pl.DeviceIdType.MESH
SETS = 2 + GQ
SW = 2 * HD
PIECES = (0, 4, 8, 12, 14, 16)
SLOTS = 2 * REACH + 4
NCH = 2
LATE = (4, 5)
SPLIT = (2, 1, 1, 1, 1, 4)
CHUNKS = 3
(S_MATE, S_LATE, S_XMATE, S_SIB, S_IDS, S_IDUP, S_IDDOWN, S_TOK, S_UP, S_DOWN, S_OUT, S_X, S_Z) = range(13)


def kernel(n_chips, tok_ref, gain_ref, wq_ref, wk_ref, wv_ref, id_ref, out_ref,
           gain, ids_in, starts, xraw, xn, wk_in, wv_in, wq_in, wbuf, qbuf, win, idwin, obuf,
           send_sem, loc_sem, init_sem, late_sem, mate_sem, zsem, xsem, tok_sem, id_sem, halo_sem, out_sem):
    nz = n_chips // 2
    rows, width = tok_ref.shape
    g = lax.axis_index("groups")
    s = lax.axis_index("seq")
    gx = lax.rem(g, 2)
    gp = g + 1 - 2 * gx
    c = lax.rem(s, 2)
    p = s // 2
    y = lax.rem(p, 2)
    z = p // 2
    me4 = 2 * y + c
    sib4 = 2 * y + 1 - c
    ys4 = 2 * (1 - y) + c
    yo4 = 2 * (1 - y) + 1 - c

    sib = (g, 4 * z + sib4)
    ysame = (g, 4 * z + ys4)
    yother = (g, 4 * z + yo4)
    twin = (gp, s)
    zm, zp = (g, s - 4), (g, s + 4)
    has_zm, has_zp = z >= 1, z + 1 < nz

    def guarded(cond, f):
        if cond is None:
            f()
        else:
            pl.when(cond)(f)

    def send(group, src, dst, rsem, dev, cond=None):
        d = pltpu.make_async_remote_copy(src_ref=src, dst_ref=dst, send_sem=send_sem.at[group],
                                         recv_sem=rsem, device_id=dev, device_id_type=MESH)
        guarded(cond, d.start)

    def recv(dst, rsem, dev, cond=None):
        d = pltpu.make_async_remote_copy(src_ref=dst, dst_ref=dst, send_sem=send_sem.at[0],
                                         recv_sem=rsem, device_id=dev, device_id_type=MESH)
        guarded(cond, d.wait_recv)

    def sent(group, like, cond=None):
        d = pltpu.make_async_remote_copy(src_ref=like, dst_ref=like, send_sem=send_sem.at[group],
                                         recv_sem=init_sem.at[0], device_id=sib, device_id_type=MESH)
        guarded(cond, d.wait_send)

    def local(src, dst, i):
        d = pltpu.make_async_copy(src, dst, loc_sem.at[i])
        d.start()
        return d

    def columns(head, i):
        return pl.ds(pl.multiple_of(head * HD if i < 2 else head * (GQ * HD) + (i - 2) * HD, HD), HD)

    weights = (wk_in, wv_in) + (wq_in,) * GQ

    def unit(t, zz, half):
        return wbuf.at[t, half, zz]

    def mates(t, half):
        return wbuf.at[t, half, z, 1 - y]

    def full_part(i, head, yy, cc):
        return weights[i].at[:, :, columns(head, i)], wbuf.at[i, :, z, yy, cc]

    def half_part(i, head, yy, cc, half):
        return weights[i].at[half, :, columns(head, i)], wbuf.at[i, half, z, yy, cc]

    loc_in = [local(src, dst, 3 + i)
              for i, (src, dst) in enumerate(((wk_ref, wk_in), (wv_ref, wv_in), (wq_ref, wq_in),
                                              (id_ref, ids_in), (gain_ref, gain)))]

    barrier = pltpu.get_barrier_semaphore()
    for dev in (sib, ysame, yother, twin):
        pl.semaphore_signal(barrier, inc=1, device_id=dev, device_id_type=MESH)
    for cond, dev in ((has_zm, zm), (has_zp, zp)):
        guarded(cond, functools.partial(pl.semaphore_signal, barrier, inc=1, device_id=dev, device_id_type=MESH))

    loc_in[3].wait()
    for i in range(NCH):
        idwin[NCH * (REACH + me4) + i] = jnp.full(idwin.shape[1:], ids_in[i] + 1, jnp.int32)
    pl.semaphore_wait(barrier, 4 + jnp.where(has_zm, 1, 0) + jnp.where(has_zp, 1, 0))

    pcuts = [rows * q // 16 for q in PIECES]
    cuts = (0, rows // 2, rows // 4 * 3, rows)
    for i in range(SETS):
        if i < 3:
            loc_in[i].wait()
        for dev, head in ((ysame, ys4), (yother, yo4)):
            a, b = half_part(i, head, y, c, gx)
            send(S_MATE, a, b, init_sem.at[1 + i], dev)
        a, b = full_part(i, sib4, y, c)
        send(S_SIB, a, b, init_sem.at[0 if SPLIT[i] == 2 else 1 + i], sib)
    for i in range(SETS):
        local(*full_part(i, me4, y, c), 0)
    loc_x = local(tok_ref, xraw.at[me4], 1)
    own_ids = idwin.at[pl.ds(NCH * (REACH + me4), NCH)]
    for dev in (sib, ysame, yother):
        send(S_IDS, own_ids, own_ids, id_sem.at[0], dev)
    for j in range(len(PIECES) - 1):
        r = slice(*pcuts[j:j + 2])
        send(S_TOK, tok_ref.at[r], xraw.at[me4, r], tok_sem.at[0, j], ysame)
    for i in LATE:
        for dev, head in ((ysame, ys4), (yother, yo4)):
            a, b = half_part(i, head, y, c, 1 - gx)
            send(S_LATE, a, b, late_sem, dev)
    send(S_TOK, tok_ref, xraw.at[me4], tok_sem.at[2, 0], sib)

    def blank(lo):
        def f():
            win[lo:lo + REACH] = jnp.zeros((REACH, rows, SW), jnp.bfloat16)
            idwin[NCH * lo:NCH * (lo + REACH)] = jnp.zeros((NCH * REACH,) + idwin.shape[1:], jnp.int32)
        return f

    def parts(t, zz, half):
        ref = unit(t, zz, half)
        if SPLIT[t] == 4:
            return [ref.at[k // 2, k % 2] for k in range(4)]
        if SPLIT[t] == 2:
            return [ref.at[y], ref.at[1 - y]]
        return [ref]

    zkeys = {}

    def z_at(*key):
        return zsem.at[zkeys.setdefault(key, len(zkeys))]

    def gather(t):
        if t == 0:
            like = wbuf.at[:, :, 0, 0, 0]
            pltpu.make_async_copy(like, like, loc_sem.at[0]).wait()
        if SPLIT[t] == 2:
            recv(full_part(t, me4, y, 1 - c)[1], init_sem.at[0], sib)
            relay_part(t, 0, 0)
            recv(wbuf.at[t, gx, z, 1 - y], init_sem.at[1 + t], ysame)
        else:
            recv(wbuf.at[t, gx, z], init_sem.at[1 + t], ysame)
        if t not in LATE:
            send(S_XMATE, mates(t, gx), mates(t, gx), mate_sem.at[t // 2], twin)

    def relay_part(t, d, k):
        for way, (zz, has, back, has_on, on) in enumerate((
                (z - d, z >= d, zm, has_zp, zp), (z + d, z + d < nz, zp, has_zm, zm))):
            ref = parts(t, zz, gx)[k]
            if d > 0:
                recv(ref, z_at(t, way, d, k), back, has)
            if d + 1 < nz:
                send(S_Z + 2 * d + way, ref, ref, z_at(t, way, d + 1, k), on, has & has_on if d > 0 else has_on)
            if d > 0:
                send(S_X, ref, ref, xsem.at[t // 2], twin, has)

    def relay(t, d):
        for k in range(SPLIT[t]):
            if d > 0 or k > 0 or SPLIT[t] != 2:
                relay_part(t, d, k)

    def finish(pair):
        if 2 * pair in LATE:
            recv(wbuf.at[2 * pair:2 * pair + 2, 1 - gx, z, 1 - y], late_sem, ysame)
        else:
            recv(wbuf.at[2 * pair:2 * pair + 2, 1 - gx, z, 1 - y], mate_sem.at[pair], twin)
        recv(wbuf.at[2 * pair:2 * pair + 2, 1 - gx, 0:nz - 1], xsem.at[pair], twin)

    def normalize(slot, first=0, count=None):
        step = 16
        count = rows if count is None else count

        def body(i, _):
            r = pl.ds(pl.multiple_of(first + i * step, step), step)
            wide = xraw[slot, r, :].astype(jnp.float32)
            inv = lax.rsqrt(jnp.mean(wide * wide, axis=-1, keepdims=True) + 1e-05)
            xn[slot, r, :] = (wide * inv * gain[...]).astype(jnp.bfloat16)
            return 0

        lax.fori_loop(0, count // step, body, 0)

    def tokens(j):
        r = slice(*pcuts[j:j + 2])
        recv(xraw.at[ys4, r], tok_sem.at[0, j], ysame)
        send(S_TOK, xraw.at[ys4, r], xraw.at[ys4, r], tok_sem.at[1, j], sib)
        normalize(ys4, r.start, r.stop - r.start)
        recv(xraw.at[yo4, r], tok_sem.at[1, j], sib)
        normalize(yo4, r.start, r.stop - r.start)

    def project(t, yy, lo, hi):
        n = hi - lo
        a = xn[pl.ds(2 * yy, 2), lo:hi, :].reshape(2 * n, width)
        w = jnp.concatenate(
            [jnp.concatenate([wbuf[2 * t + i, h, zz, yc // 2, yc % 2] for i in range(2)], axis=1)
             for zz in range(nz) for yc in range(4) for h in range(2)], axis=0)
        r = jnp.dot(a, w, preferred_element_type=jnp.float32).astype(jnp.bfloat16)
        for i in range(2):
            part = r[i * n:(i + 1) * n]
            if t == 0:
                win[REACH + 2 * yy + i, lo:hi, :] = part
            else:
                for h in range(2):
                    qbuf[t - 1, 2 * yy + i, lo // HD, h] = part[:, h * HD:(h + 1) * HD]

    def halo_send(yy, ch):
        r = slice(*cuts[ch:ch + 2])
        for slot in range(4):
            mine = (slot // 2) == yy
            a = win.at[REACH + slot, r]
            if slot > 0:
                send(S_UP, a, win.at[slot - 1, r], halo_sem.at[0], zp, mine & has_zp)
            if slot < 3:
                send(S_DOWN, a, win.at[REACH + 4 + slot, r], halo_sem.at[1], zm, mine & has_zm)

    def halo_recv():
        recv(win.at[0:REACH], halo_sem.at[0], zm, has_zm)
        recv(win.at[REACH + 4:SLOTS], halo_sem.at[1], zp, has_zp)

    def ids_send():
        recv(idwin.at[0:3 * NCH], id_sem.at[0], sib)
        edge = NCH * REACH
        a = NCH * (REACH + 4)
        send(S_IDUP, idwin.at[a - edge:a], idwin.at[0:edge], id_sem.at[1], zp, has_zp)
        send(S_IDDOWN, idwin.at[edge:2 * edge], idwin.at[a:a + edge], id_sem.at[2], zm, has_zm)

    def ids_recv():
        edge = NCH * REACH
        a = NCH * (REACH + 4)
        recv(idwin.at[0:edge], id_sem.at[1], zm, has_zm)
        recv(idwin.at[a:a + edge], id_sem.at[2], zp, has_zp)
        lane = lax.broadcasted_iota(jnp.int32, (8, HD), 1)
        ids = jnp.zeros((8, HD), jnp.int32)
        for j in range(SLOTS * NCH):
            ids = jnp.where(lane == j, idwin[j], ids)
        for j in range(edge, a):
            opening = jnp.min(jnp.where(ids == idwin[j], lane, j))
            starts[j - edge] = jnp.maximum(opening, j - edge)

    rate = HD ** (-0.5) * math.log2(math.e)
    span = REACH * NCH + 1

    def attend(slot, t):
        kv = win.reshape(SLOTS * NCH, HD, SW)
        for qb in range(NCH):
            mine = idwin[NCH * (REACH + slot) + qb, 0:1, :]
            start = starts[NCH * slot + qb]
            bias = jnp.concatenate(
                [jnp.where(idwin[start + j, 0:1, :] == mine, 0.0, -1e30) for j in range(span)], axis=1)
            q = qbuf[t, slot, qb].reshape(2 * HD, HD)
            at = pl.ds(start, span)
            k = kv[at, :, 0:HD].reshape(span * HD, HD)
            v = jnp.concatenate([kv[at, :, HD:SW].reshape(span * HD, HD),
                                 jnp.ones((span * HD, HD), jnp.bfloat16)], axis=1)
            sc = lax.dot_general(q, k, (((1,), (1,)), ((), ())), preferred_element_type=jnp.float32) + bias
            top = jnp.max(sc, axis=-1, keepdims=True)
            w = jnp.exp2((sc - top) * rate).astype(jnp.bfloat16)
            o = jnp.dot(w, v, preferred_element_type=jnp.float32)
            o = (o[:, 0:HD] / o[:, HD:SW]).astype(jnp.bfloat16)
            rr = slice(qb * HD, (qb + 1) * HD)
            obuf[t, slot, rr, 0:HD] = o[0:HD]
            obuf[t, slot, rr, HD:SW] = o[HD:SW]

    def out_cols(head, t):
        return out_ref.at[:, pl.ds(pl.multiple_of(head * (GQ * HD) + t * SW, HD), SW)]

    def attend_slots(t, group):
        for i, slot, dev in group:
            attend(slot, t)
            src = obuf.at[t, slot]
            if dev is None:
                local(src, out_cols(me4, t), 2)
            else:
                send(S_OUT, src, out_cols(me4, t), out_sem, dev)

    last = nz - 1
    held = ((5, last - 1), (4, last), (5, last))
    order = sorted(((t, d) for t in range(SETS) for d in range(nz) if (t, d) not in held),
                   key=lambda td: (nz - 1) * td[0] + (nz - 0.5) * td[1])
    after = {}

    def at_task(index, f):
        after.setdefault(min(index, len(order) - 1), []).append(f)

    def kv_early():
        finish(0)
        project(0, y, 0, HD)
        project(0, y, HD, rows)
        project(0, 1 - y, 0, HD)
        halo_send(1 - y, 0)

    def kv_more():
        tokens(2)
        project(0, 1 - y, *cuts[1:3])
        halo_send(1 - y, 1)
        for ch in range(CHUNKS):
            halo_send(y, ch)

    def own_tokens():
        loc_x.wait()
        loc_in[4].wait()
        normalize(me4)

    def sib_tokens():
        recv(xraw.at[sib4], tok_sem.at[2, 0], sib)
        normalize(sib4)
        pl.when(z < 1)(blank(0))
        pl.when(z + 1 >= nz)(blank(REACH + 4))

    at_task(order.index((2, 0)), own_tokens)
    at_task(order.index((3, 0)), ids_send)
    at_task(order.index((3, 0)), sib_tokens)
    at_task(order.index((0, last)), lambda: tokens(0))
    at_task(order.index((4, 1)), lambda: tokens(1))
    at_task(order.index((1, last)) + 2, kv_early)
    at_task(max(order.index((4, min(2, last))), order.index((1, last)) + 3), kv_more)
    gathered = 0
    for i, (t, d) in enumerate(order):
        while gathered < SETS and (gathered <= t or d > 0 or gathered <= i + 1):
            gather(gathered)
            gathered += 1
        relay(t, d)
        for f in after.get(i, ()):
            f()
    tokens(3)
    tokens(4)
    project(0, 1 - y, *cuts[2:4])
    halo_send(1 - y, 2)
    relay(*held[0])
    relay(*held[1])
    finish(1)
    for yy in (1 - y, y):
        project(1, yy, 0, HD)
        project(1, yy, HD, rows)
    ids_recv()
    halo_recv()
    far = ((0, yo4, yother), (1, ys4, ysame))
    near = ((2, sib4, sib), (3, me4, None))
    attend_slots(0, far)
    relay(*held[2])
    attend_slots(0, near)
    finish(2)
    project(2, 1 - y, 0, HD)
    project(2, 1 - y, HD, rows)
    attend_slots(1, far)
    project(2, y, 0, HD)
    project(2, y, HD, rows)
    attend_slots(1, near)
    recv(obuf.at[:, 0:3], out_sem, sib)
    pltpu.make_async_copy(obuf.at[:, 0], obuf.at[:, 0], loc_sem.at[2]).wait()
    sent(S_MATE, wbuf.at[:, 0, 0, 0])
    sent(S_LATE, wbuf.at[0:len(LATE), 0, 0, 0])
    sent(S_XMATE, wbuf.at[0:SETS - len(LATE), 0, 0, 0])
    sent(S_SIB, wbuf.at[:, :, 0, 0, 0])
    sent(S_IDS, idwin.at[0:3 * NCH])
    sent(S_IDUP, idwin.at[0:NCH * REACH], has_zp)
    sent(S_IDDOWN, idwin.at[0:NCH * REACH], has_zm)
    sent(S_TOK, xraw.at[0:3])
    sent(S_UP, win.at[0:REACH], has_zp)
    sent(S_DOWN, win.at[0:REACH], has_zm)
    sent(S_OUT, obuf.at[:, 0:3])
    sent(S_X, wbuf.at[:, 0, 0:nz - 1])
    for d in range(nz - 1):
        sent(S_Z + 2 * d, wbuf.at[:, 0, 0], has_zp & (z >= d))
        sent(S_Z + 2 * d + 1, wbuf.at[:, 0, 0], has_zm & (z + d < nz))


def solution(mesh):
    n_seq = mesh.shape["seq"]
    n_chips = n_seq // 2
    nz = n_chips // 2

    def on_device(tokens, norm_gain, w_query, w_key, w_value, passage_blocks):
        rows, width = tokens.shape
        anywhere = pl.BlockSpec(memory_space=pl.ANY)
        hbm = pl.BlockSpec(memory_space=pltpu.HBM)
        bf = jnp.bfloat16
        dma = pltpu.SemaphoreType.DMA
        half = w_query.shape[0] // 2
        halves = [w.reshape(2, half, w.shape[1]) for w in (w_query, w_key, w_value)]
        return pl.pallas_call(
            functools.partial(kernel, n_chips),
            out_shape=jax.ShapeDtypeStruct((rows, QH * HD), bf),
            in_specs=[hbm] * 6,
            out_specs=anywhere,
            scratch_shapes=[
                pltpu.VMEM((1, width), jnp.float32),
                pltpu.SMEM(passage_blocks.shape, jnp.int32),
                pltpu.SMEM((4 * NCH,), jnp.int32),
                pltpu.VMEM((4, rows, width), bf),
                pltpu.VMEM((4, rows, width), bf),
                *(pltpu.VMEM((2, half, w.shape[1]), bf) for w in (w_key, w_value, w_query)),
                pltpu.VMEM((SETS, 2, nz, 2, 2, half, HD), bf),
                pltpu.VMEM((2, 4, NCH, 2, HD, HD), bf),
                pltpu.VMEM((SLOTS, rows, SW), bf),
                pltpu.VMEM((SLOTS * NCH, 8, HD), jnp.int32),
                pltpu.VMEM((2, 4, rows, SW), bf),
                dma((S_Z + 2 * (nz - 1),)), dma((8,)), dma((1 + SETS,)), dma, dma((2,)),
                dma((sum(SPLIT) * 2 * (nz - 1),)), dma((3,)), dma((3, len(PIECES) - 1)), dma((3,)), dma((2,)), dma,
            ],
            compiler_params=pltpu.CompilerParams(
                collective_id=0, has_side_effects=True, vmem_limit_bytes=52 * 2**20),
        )(*(pltpu.with_memory_space_constraint(a, pltpu.HBM)
            for a in (tokens, norm_gain[None, :], *halves, passage_blocks)))

    in_specs = (
        P(("groups", "seq"), None),
        P(),
        P("seq", None),
        P("seq", None),
        P("seq", None),
        P(("groups", "seq")),
    )
    out_specs = P(("groups", "seq"), None)
    return jax.shard_map(on_device, mesh=mesh, in_specs=in_specs, out_specs=out_specs, check_vma=False)
```

```python
import functools
import math

import jax
import jax.numpy as jnp
from jax import lax
from jax.experimental import pallas as pl
from jax.experimental.pallas import tpu as pltpu
from jax.sharding import PartitionSpec as P

HD = 128
QH = 16
KVH = 4
REACH = 3
GQ = QH // KVH
MESH = pl.DeviceIdType.MESH
SETS = 2 + GQ
SW = 2 * HD
PIECES = (0, 4, 8, 12, 14, 15, 16)
SLOTS = 2 * REACH + 4
NCH = 2
LATE = (4, 5)
SPLIT = (2, 1, 1, 1, 1, 4)
(S_MATE, S_LATE, S_XMATE, S_SIB, S_IDS, S_IDUP, S_IDDOWN, S_TOK, S_UP, S_DOWN, S_OUT, S_X, S_Z) = range(13)


def kernel(n_chips, tok_ref, gain_ref, wq_ref, wk_ref, wv_ref, id_ref, out_ref,
           gain, ids_in, starts, xraw, xn, wk_in, wv_in, wq_in, wbuf, qbuf, win, idwin, obuf,
           send_sem, loc_sem, init_sem, late_sem, mate_sem, zsem, xsem, tok_sem, id_sem, halo_sem, out_sem):
    nz = n_chips // 2
    rows, width = tok_ref.shape
    g = lax.axis_index("groups")
    s = lax.axis_index("seq")
    gx = lax.rem(g, 2)
    gp = g + 1 - 2 * gx
    c = lax.rem(s, 2)
    p = s // 2
    y = lax.rem(p, 2)
    z = p // 2
    me4 = 2 * y + c
    sib4 = 2 * y + 1 - c
    ys4 = 2 * (1 - y) + c
    yo4 = 2 * (1 - y) + 1 - c

    sib = (g, 4 * z + sib4)
    ysame = (g, 4 * z + ys4)
    yother = (g, 4 * z + yo4)
    twin = (gp, s)
    zm, zp = (g, s - 4), (g, s + 4)
    has_zm, has_zp = z >= 1, z + 1 < nz

    def guarded(cond, f):
        if cond is None:
            f()
        else:
            pl.when(cond)(f)

    def send(group, src, dst, rsem, dev, cond=None):
        d = pltpu.make_async_remote_copy(src_ref=src, dst_ref=dst, send_sem=send_sem.at[group],
                                         recv_sem=rsem, device_id=dev, device_id_type=MESH)
        guarded(cond, d.start)

    def recv(dst, rsem, dev, cond=None):
        d = pltpu.make_async_remote_copy(src_ref=dst, dst_ref=dst, send_sem=send_sem.at[0],
                                         recv_sem=rsem, device_id=dev, device_id_type=MESH)
        guarded(cond, d.wait_recv)

    def sent(group, like, cond=None):
        d = pltpu.make_async_remote_copy(src_ref=like, dst_ref=like, send_sem=send_sem.at[group],
                                         recv_sem=init_sem.at[0], device_id=sib, device_id_type=MESH)
        guarded(cond, d.wait_send)

    def local(src, dst, i):
        d = pltpu.make_async_copy(src, dst, loc_sem.at[i])
        d.start()
        return d

    def columns(head, i):
        return pl.ds(pl.multiple_of(head * HD if i < 2 else head * (GQ * HD) + (i - 2) * HD, HD), HD)

    weights = (wk_in, wv_in) + (wq_in,) * GQ

    def unit(t, zz, half):
        return wbuf.at[t, half, zz]

    def mates(t, half):
        return wbuf.at[t, half, z, 1 - y]

    def full_part(i, head, yy, cc):
        return weights[i].at[:, :, columns(head, i)], wbuf.at[i, :, z, yy, cc]

    def half_part(i, head, yy, cc, half):
        return weights[i].at[half, :, columns(head, i)], wbuf.at[i, half, z, yy, cc]

    loc_in = [local(src, dst, 3 + i)
              for i, (src, dst) in enumerate(((wk_ref, wk_in), (wv_ref, wv_in), (wq_ref, wq_in),
                                              (id_ref, ids_in), (gain_ref, gain)))]

    barrier = pltpu.get_barrier_semaphore()
    for dev in (sib, ysame, yother, twin):
        pl.semaphore_signal(barrier, inc=1, device_id=dev, device_id_type=MESH)
    for cond, dev in ((has_zm, zm), (has_zp, zp)):
        guarded(cond, functools.partial(pl.semaphore_signal, barrier, inc=1, device_id=dev, device_id_type=MESH))

    loc_in[3].wait()
    for i in range(NCH):
        idwin[NCH * (REACH + me4) + i] = jnp.full(idwin.shape[1:], ids_in[i] + 1, jnp.int32)
    pl.semaphore_wait(barrier, 4 + jnp.where(has_zm, 1, 0) + jnp.where(has_zp, 1, 0))

    pcuts = [rows * q // 16 for q in PIECES]
    half, quarter, eighth = rows // 2, rows // 4 * 3, rows // 8 * 7
    for i in range(SETS):
        if i < 3:
            loc_in[i].wait()
        for dev, head in ((ysame, ys4), (yother, yo4)):
            a, b = half_part(i, head, y, c, gx)
            send(S_MATE, a, b, init_sem.at[1 + i], dev)
        a, b = full_part(i, sib4, y, c)
        send(S_SIB, a, b, init_sem.at[0 if SPLIT[i] == 2 else 1 + i], sib)
    for i in range(SETS):
        local(*full_part(i, me4, y, c), 0)
    loc_x = local(tok_ref, xraw.at[me4], 1)
    own_ids = idwin.at[pl.ds(NCH * (REACH + me4), NCH)]
    for dev in (sib, ysame, yother):
        send(S_IDS, own_ids, own_ids, id_sem.at[0], dev)
    for j in range(len(PIECES) - 1):
        r = slice(*pcuts[j:j + 2])
        send(S_TOK, tok_ref.at[r], xraw.at[me4, r], tok_sem.at[0, j], ysame)
    for i in LATE:
        for dev, head in ((ysame, ys4), (yother, yo4)):
            a, b = half_part(i, head, y, c, 1 - gx)
            send(S_LATE, a, b, late_sem, dev)
    send(S_TOK, tok_ref, xraw.at[me4], tok_sem.at[2, 0], sib)

    def blank(lo):
        def f():
            win[lo:lo + REACH] = jnp.zeros((REACH, rows, SW), jnp.bfloat16)
            idwin[NCH * lo:NCH * (lo + REACH)] = jnp.zeros((NCH * REACH,) + idwin.shape[1:], jnp.int32)
        return f

    def parts(t, zz, half):
        ref = unit(t, zz, half)
        if SPLIT[t] == 4:
            return [ref.at[k // 2, k % 2] for k in range(4)]
        if SPLIT[t] == 2:
            return [ref.at[y], ref.at[1 - y]]
        return [ref]

    zkeys = {}

    def z_at(*key):
        t, way, d, k = key
        return zsem.at[zkeys.setdefault((t, way if 2 * d < nz else 0, d, k), len(zkeys))]

    def gather(t):
        if t == 0:
            like = wbuf.at[:, :, 0, 0, 0]
            pltpu.make_async_copy(like, like, loc_sem.at[0]).wait()
        if SPLIT[t] == 2:
            recv(full_part(t, me4, y, 1 - c)[1], init_sem.at[0], sib)
            relay_part(t, 0, 0)
            recv(wbuf.at[t, gx, z, 1 - y], init_sem.at[1 + t], ysame)
        else:
            recv(wbuf.at[t, gx, z], init_sem.at[1 + t], ysame)
        if t not in LATE:
            send(S_XMATE, mates(t, gx), mates(t, gx), mate_sem.at[t // 2], twin)

    def relay_part(t, d, k):
        for way, (zz, has, back, has_on, on) in enumerate((
                (z - d, z >= d, zm, has_zp, zp), (z + d, z + d < nz, zp, has_zm, zm))):
            ref = parts(t, zz, gx)[k]
            if d > 0:
                recv(ref, z_at(t, way, d, k), back, has)
            if d + 1 < nz:
                send(S_Z + 2 * d + way, ref, ref, z_at(t, way, d + 1, k), on, has & has_on if d > 0 else has_on)
            if d > 0:
                send(S_X, ref, ref, xsem.at[t // 2], twin, has)

    def relay(t, d):
        for k in range(SPLIT[t]):
            if d > 0 or k > 0 or SPLIT[t] != 2:
                relay_part(t, d, k)

    def finish(pair):
        if 2 * pair in LATE:
            recv(wbuf.at[2 * pair:2 * pair + 2, 1 - gx, z, 1 - y], late_sem, ysame)
        else:
            recv(wbuf.at[2 * pair:2 * pair + 2, 1 - gx, z, 1 - y], mate_sem.at[pair], twin)
        recv(wbuf.at[2 * pair:2 * pair + 2, 1 - gx, 0:nz - 1], xsem.at[pair], twin)

    def normalize(slot, first=0, count=None):
        step = 16
        count = rows if count is None else count

        def body(i, _):
            r = pl.ds(pl.multiple_of(first + i * step, step), step)
            wide = xraw[slot, r, :].astype(jnp.float32)
            inv = lax.rsqrt(jnp.mean(wide * wide, axis=-1, keepdims=True) + 1e-05)
            xn[slot, r, :] = (wide * inv * gain[...]).astype(jnp.bfloat16)
            return 0

        lax.fori_loop(0, count // step, body, 0)

    def tokens(j):
        r = slice(*pcuts[j:j + 2])
        recv(xraw.at[ys4, r], tok_sem.at[0, j], ysame)
        send(S_TOK, xraw.at[ys4, r], xraw.at[ys4, r], tok_sem.at[1, j], sib)
        normalize(ys4, r.start, r.stop - r.start)
        recv(xraw.at[yo4, r], tok_sem.at[1, j], sib)
        normalize(yo4, r.start, r.stop - r.start)

    def project(t, yy, lo, hi):
        n = hi - lo
        a = xn[pl.ds(2 * yy, 2), lo:hi, :].reshape(2 * n, width)
        w = jnp.concatenate(
            [jnp.concatenate([wbuf[2 * t + i, h, zz, yc // 2, yc % 2] for i in range(2)], axis=1)
             for zz in range(nz) for yc in range(4) for h in range(2)], axis=0)
        r = jnp.dot(a, w, preferred_element_type=jnp.float32).astype(jnp.bfloat16)
        for i in range(2):
            part = r[i * n:(i + 1) * n]
            if t == 0:
                win[REACH + 2 * yy + i, lo:hi, :] = part
            else:
                for h in range(2):
                    qbuf[t - 1, 2 * yy + i, lo // HD, h] = part[:, h * HD:(h + 1) * HD]

    def halo_send(yy, lo, hi):
        r = slice(lo, hi)
        for slot in range(4):
            mine = (slot // 2) == yy
            a = win.at[REACH + slot, r]
            if slot > 0:
                send(S_UP, a, win.at[slot - 1, r], halo_sem.at[0], zp, mine & has_zp)
            if slot < 3:
                send(S_DOWN, a, win.at[REACH + 4 + slot, r], halo_sem.at[1], zm, mine & has_zm)

    def halo_recv():
        recv(win.at[0:REACH], halo_sem.at[0], zm, has_zm)
        recv(win.at[REACH + 4:SLOTS], halo_sem.at[1], zp, has_zp)

    def ids_send():
        recv(idwin.at[0:3 * NCH], id_sem.at[0], sib)
        edge = NCH * REACH
        a = NCH * (REACH + 4)
        send(S_IDUP, idwin.at[a - edge:a], idwin.at[0:edge], id_sem.at[1], zp, has_zp)
        send(S_IDDOWN, idwin.at[edge:2 * edge], idwin.at[a:a + edge], id_sem.at[2], zm, has_zm)

    def ids_recv():
        edge = NCH * REACH
        a = NCH * (REACH + 4)
        recv(idwin.at[0:edge], id_sem.at[1], zm, has_zm)
        recv(idwin.at[a:a + edge], id_sem.at[2], zp, has_zp)
        lane = lax.broadcasted_iota(jnp.int32, (8, HD), 1)
        ids = jnp.zeros((8, HD), jnp.int32)
        for j in range(SLOTS * NCH):
            ids = jnp.where(lane == j, idwin[j], ids)
        for j in range(edge, a):
            opening = jnp.min(jnp.where(ids == idwin[j], lane, j))
            starts[j - edge] = jnp.maximum(opening, j - edge)

    rate = HD ** (-0.5) * math.log2(math.e)
    span = REACH * NCH + 1

    def attend(slot, t):
        kv = win.reshape(SLOTS * NCH, HD, SW)
        for qb in range(NCH):
            mine = idwin[NCH * (REACH + slot) + qb, 0:1, :]
            start = starts[NCH * slot + qb]
            bias = jnp.concatenate(
                [jnp.where(idwin[start + j, 0:1, :] == mine, 0.0, -1e30) for j in range(span)], axis=1)
            q = qbuf[t, slot, qb].reshape(2 * HD, HD)
            at = pl.ds(start, span)
            k = kv[at, :, 0:HD].reshape(span * HD, HD)
            v = jnp.concatenate([kv[at, :, HD:SW].reshape(span * HD, HD),
                                 jnp.ones((span * HD, HD), jnp.bfloat16)], axis=1)
            sc = lax.dot_general(q, k, (((1,), (1,)), ((), ())), preferred_element_type=jnp.float32) + bias
            top = jnp.max(sc, axis=-1, keepdims=True)
            w = jnp.exp2((sc - top) * rate).astype(jnp.bfloat16)
            o = jnp.dot(w, v, preferred_element_type=jnp.float32)
            o = (o[:, 0:HD] / o[:, HD:SW]).astype(jnp.bfloat16)
            rr = slice(qb * HD, (qb + 1) * HD)
            obuf[t, slot, rr, 0:HD] = o[0:HD]
            obuf[t, slot, rr, HD:SW] = o[HD:SW]

    def out_cols(head, t):
        return out_ref.at[:, pl.ds(pl.multiple_of(head * (GQ * HD) + t * SW, HD), SW)]

    def attend_slots(t, group):
        for i, slot, dev in group:
            attend(slot, t)
            src = obuf.at[t, slot]
            if dev is None:
                local(src, out_cols(me4, t), 2)
            else:
                send(S_OUT, src, out_cols(me4, t), out_sem, dev)

    last = nz - 1
    held = ((5, last - 1), (4, last), (5, last))
    order = sorted(((t, d) for t in range(SETS) for d in range(nz) if (t, d) not in held),
                   key=lambda td: (nz - 1) * td[0] + (nz - 0.5) * td[1])
    after = {}

    def at_task(index, f):
        after.setdefault(min(index, len(order) - 1), []).append(f)

    def kv_early():
        finish(0)
        project(0, y, 0, HD)
        project(0, y, HD, rows)
        project(0, 1 - y, 0, HD)
        halo_send(1 - y, 0, half)

    def kv_more():
        tokens(2)
        project(0, 1 - y, half, quarter)
        halo_send(1 - y, half, quarter)
        halo_send(y, 0, rows)

    def own_tokens():
        loc_x.wait()
        loc_in[4].wait()
        normalize(me4)

    def sib_tokens():
        recv(xraw.at[sib4], tok_sem.at[2, 0], sib)
        normalize(sib4)
        pl.when(z < 1)(blank(0))
        pl.when(z + 1 >= nz)(blank(REACH + 4))

    at_task(order.index((2, 0)), own_tokens)
    at_task(order.index((3, 0)), ids_send)
    at_task(order.index((3, 0)), sib_tokens)
    at_task(order.index((0, last)), lambda: tokens(0))
    at_task(order.index((4, 1)), lambda: tokens(1))
    at_task(order.index((1, last)) + 2, kv_early)
    at_task(max(order.index((4, min(2, last))), order.index((1, last)) + 3), kv_more)
    gathered = moved = 0
    for i, (t, d) in enumerate(order):
        moved += d > 0
        while gathered < SETS and gathered <= max(t, moved + 1 if moved else 0):
            gather(gathered)
            gathered += 1
        relay(t, d)
        for f in after.get(i, ()):
            f()
    tokens(3)
    project(0, 1 - y, quarter, eighth)
    halo_send(1 - y, quarter, eighth)
    tokens(4)
    tokens(5)
    project(0, 1 - y, eighth, rows)
    halo_send(1 - y, eighth, rows)
    relay(*held[0])
    relay(*held[1])
    finish(1)
    for yy in (1 - y, y):
        project(1, yy, 0, HD)
        project(1, yy, HD, rows)
    ids_recv()
    halo_recv()
    far = ((0, yo4, yother), (1, ys4, ysame))
    near = ((2, sib4, sib), (3, me4, None))
    attend_slots(0, far)
    relay(*held[2])
    attend_slots(0, near)
    finish(2)
    project(2, 1 - y, 0, HD)
    project(2, 1 - y, HD, rows)
    attend_slots(1, far)
    project(2, y, 0, HD)
    project(2, y, HD, rows)
    attend_slots(1, near)
    recv(obuf.at[:, 0:3], out_sem, sib)
    pltpu.make_async_copy(obuf.at[:, 0], obuf.at[:, 0], loc_sem.at[2]).wait()
    sent(S_MATE, wbuf.at[:, 0, 0, 0])
    sent(S_LATE, wbuf.at[0:len(LATE), 0, 0, 0])
    sent(S_XMATE, wbuf.at[0:SETS - len(LATE), 0, 0, 0])
    sent(S_SIB, wbuf.at[:, :, 0, 0, 0])
    sent(S_IDS, idwin.at[0:3 * NCH])
    sent(S_IDUP, idwin.at[0:NCH * REACH], has_zp)
    sent(S_IDDOWN, idwin.at[0:NCH * REACH], has_zm)
    sent(S_TOK, xraw.at[0:3])
    sent(S_UP, win.at[0:REACH], has_zp)
    sent(S_DOWN, win.at[0:REACH], has_zm)
    sent(S_OUT, obuf.at[:, 0:3])
    sent(S_X, wbuf.at[:, 0, 0:nz - 1])
    for d in range(nz - 1):
        sent(S_Z + 2 * d, wbuf.at[:, 0, 0], has_zp & (z >= d))
        sent(S_Z + 2 * d + 1, wbuf.at[:, 0, 0], has_zm & (z + d < nz))


def solution(mesh):
    n_seq = mesh.shape["seq"]
    n_chips = n_seq // 2
    nz = n_chips // 2

    def on_device(tokens, norm_gain, w_query, w_key, w_value, passage_blocks):
        rows, width = tokens.shape
        anywhere = pl.BlockSpec(memory_space=pl.ANY)
        hbm = pl.BlockSpec(memory_space=pltpu.HBM)
        bf = jnp.bfloat16
        dma = pltpu.SemaphoreType.DMA
        half = w_query.shape[0] // 2
        halves = [w.reshape(2, half, w.shape[1]) for w in (w_query, w_key, w_value)]
        return pl.pallas_call(
            functools.partial(kernel, n_chips),
            out_shape=jax.ShapeDtypeStruct((rows, QH * HD), bf),
            in_specs=[hbm] * 6,
            out_specs=anywhere,
            scratch_shapes=[
                pltpu.VMEM((1, width), jnp.float32),
                pltpu.SMEM(passage_blocks.shape, jnp.int32),
                pltpu.SMEM((4 * NCH,), jnp.int32),
                pltpu.VMEM((4, rows, width), bf),
                pltpu.VMEM((4, rows, width), bf),
                *(pltpu.VMEM((2, half, w.shape[1]), bf) for w in (w_key, w_value, w_query)),
                pltpu.VMEM((SETS, 2, nz, 2, 2, half, HD), bf),
                pltpu.VMEM((2, 4, NCH, 2, HD, HD), bf),
                pltpu.VMEM((SLOTS, rows, SW), bf),
                pltpu.VMEM((SLOTS * NCH, 8, HD), jnp.int32),
                pltpu.VMEM((2, 4, rows, SW), bf),
                dma((S_Z + 2 * (nz - 1),)), dma((8,)), dma((1 + SETS,)), dma, dma((2,)),
                dma((sum(SPLIT) * sum(2 if 2 * d < nz else 1 for d in range(1, nz)),)), dma((3,)), dma((3, len(PIECES) - 1)), dma((3,)), dma((2,)), dma,
            ],
            compiler_params=pltpu.CompilerParams(
                collective_id=0, has_side_effects=True, vmem_limit_bytes=52 * 2**20),
        )(*(pltpu.with_memory_space_constraint(a, pltpu.HBM)
            for a in (tokens, norm_gain[None, :], *halves, passage_blocks)))

    in_specs = (
        P(("groups", "seq"), None),
        P(),
        P("seq", None),
        P("seq", None),
        P("seq", None),
        P(("groups", "seq")),
    )
    out_specs = P(("groups", "seq"), None)
    return jax.shard_map(on_device, mesh=mesh, in_specs=in_specs, out_specs=out_specs, check_vma=False)
```

```python
import functools
import math

import jax
import jax.numpy as jnp
from jax import lax
from jax.experimental import pallas as pl
from jax.experimental.pallas import tpu as pltpu
from jax.sharding import PartitionSpec as P

HD = 128
QH = 16
KVH = 4
REACH = 3
GQ = QH // KVH
MESH = pl.DeviceIdType.MESH
SETS = 2 + GQ
SW = 2 * HD
PIECES = (0, 4, 8, 12, 14, 15, 16)
SLOTS = 2 * REACH + 4
NCH = 2
LATE = (4, 5)
SPLIT = (2, 1, 1, 1, 1, 4)
(S_MATE, S_LATE, S_XMATE, S_SIB, S_IDS, S_IDUP, S_IDDOWN, S_TOK, S_UP, S_DOWN, S_OUT, S_X, S_Z) = range(13)


def kernel(n_chips, tok_ref, gain_ref, wq_ref, wk_ref, wv_ref, id_ref, out_ref,
           gain, ids_in, starts, xraw, xn, wk_in, wv_in, wq_in, wbuf, qbuf, win, idwin, obuf,
           send_sem, loc_sem, init_sem, late_sem, mate_sem, zsem, xsem, tok_sem, id_sem, halo_sem, out_sem):
    nz = n_chips // 2
    rows, width = tok_ref.shape
    g = lax.axis_index("groups")
    s = lax.axis_index("seq")
    gx = lax.rem(g, 2)
    gp = g + 1 - 2 * gx
    c = lax.rem(s, 2)
    p = s // 2
    y = lax.rem(p, 2)
    z = p // 2
    me4 = 2 * y + c
    sib4 = 2 * y + 1 - c
    ys4 = 2 * (1 - y) + c
    yo4 = 2 * (1 - y) + 1 - c

    sib = (g, 4 * z + sib4)
    ysame = (g, 4 * z + ys4)
    yother = (g, 4 * z + yo4)
    twin = (gp, s)
    zm, zp = (g, s - 4), (g, s + 4)
    has_zm, has_zp = z >= 1, z + 1 < nz

    def guarded(cond, f):
        if cond is None:
            f()
        else:
            pl.when(cond)(f)

    def send(group, src, dst, rsem, dev, cond=None):
        d = pltpu.make_async_remote_copy(src_ref=src, dst_ref=dst, send_sem=send_sem.at[group],
                                         recv_sem=rsem, device_id=dev, device_id_type=MESH)
        guarded(cond, d.start)

    def recv(dst, rsem, dev, cond=None):
        d = pltpu.make_async_remote_copy(src_ref=dst, dst_ref=dst, send_sem=send_sem.at[0],
                                         recv_sem=rsem, device_id=dev, device_id_type=MESH)
        guarded(cond, d.wait_recv)

    def sent(group, like, cond=None):
        d = pltpu.make_async_remote_copy(src_ref=like, dst_ref=like, send_sem=send_sem.at[group],
                                         recv_sem=init_sem.at[0], device_id=sib, device_id_type=MESH)
        guarded(cond, d.wait_send)

    def local(src, dst, i):
        d = pltpu.make_async_copy(src, dst, loc_sem.at[i])
        d.start()
        return d

    def columns(head, i):
        return pl.ds(pl.multiple_of(head * HD if i < 2 else head * (GQ * HD) + (i - 2) * HD, HD), HD)

    weights = (wk_in, wv_in) + (wq_in,) * GQ

    def unit(t, zz, half):
        return wbuf.at[t, half, zz]

    def mates(t, half):
        return wbuf.at[t, half, z, 1 - y]

    def full_part(i, head, yy, cc):
        return weights[i].at[:, :, columns(head, i)], wbuf.at[i, :, z, yy, cc]

    def half_part(i, head, yy, cc, half):
        return weights[i].at[half, :, columns(head, i)], wbuf.at[i, half, z, yy, cc]

    loc_in = [local(src, dst, 3 + i)
              for i, (src, dst) in enumerate(((wk_ref, wk_in), (wv_ref, wv_in), (wq_ref, wq_in),
                                              (id_ref, ids_in), (gain_ref, gain)))]

    barrier = pltpu.get_barrier_semaphore()
    for dev in (sib, ysame, yother, twin):
        pl.semaphore_signal(barrier, inc=1, device_id=dev, device_id_type=MESH)
    for cond, dev in ((has_zm, zm), (has_zp, zp)):
        guarded(cond, functools.partial(pl.semaphore_signal, barrier, inc=1, device_id=dev, device_id_type=MESH))

    loc_in[3].wait()
    for i in range(NCH):
        idwin[NCH * (REACH + me4) + i] = jnp.full(idwin.shape[1:], ids_in[i] + 1, jnp.int32)
    pl.semaphore_wait(barrier, 4 + jnp.where(has_zm, 1, 0) + jnp.where(has_zp, 1, 0))

    pcuts = [rows * q // 16 for q in PIECES]
    half, quarter, eighth = rows // 2, rows // 4 * 3, rows // 8 * 7
    for i in range(SETS):
        if i < 3:
            loc_in[i].wait()
        for dev, head in ((ysame, ys4), (yother, yo4)):
            a, b = half_part(i, head, y, c, gx)
            send(S_MATE, a, b, init_sem.at[1 + i], dev)
        a, b = full_part(i, sib4, y, c)
        send(S_SIB, a, b, init_sem.at[0 if SPLIT[i] == 2 else 1 + i], sib)
    for i in range(SETS):
        local(*full_part(i, me4, y, c), 0)
    loc_x = local(tok_ref, xraw.at[me4], 1)
    own_ids = idwin.at[pl.ds(NCH * (REACH + me4), NCH)]
    for dev in (sib, ysame, yother):
        send(S_IDS, own_ids, own_ids, id_sem.at[0], dev)
    for j in range(len(PIECES) - 1):
        r = slice(*pcuts[j:j + 2])
        send(S_TOK, tok_ref.at[r], xraw.at[me4, r], tok_sem.at[0, j], ysame)
    for i in LATE:
        for dev, head in ((ysame, ys4), (yother, yo4)):
            a, b = half_part(i, head, y, c, 1 - gx)
            send(S_LATE, a, b, late_sem, dev)
    send(S_TOK, tok_ref, xraw.at[me4], tok_sem.at[2, 0], sib)

    def blank(lo):
        def f():
            win[lo:lo + REACH] = jnp.zeros((REACH, rows, SW), jnp.bfloat16)
            idwin[NCH * lo:NCH * (lo + REACH)] = jnp.zeros((NCH * REACH,) + idwin.shape[1:], jnp.int32)
        return f

    def parts(t, zz, half):
        ref = unit(t, zz, half)
        if SPLIT[t] == 4:
            return [ref.at[k // 2, k % 2] for k in range(4)]
        if SPLIT[t] == 2:
            return [ref.at[y], ref.at[1 - y]]
        return [ref]

    zkeys = {}

    def z_at(*key):
        t, way, d, k = key
        return zsem.at[zkeys.setdefault((t, way if 2 * d < nz else 0, d, k), len(zkeys))]

    def gather(t):
        if t == 0:
            like = wbuf.at[:, :, 0, 0, 0]
            pltpu.make_async_copy(like, like, loc_sem.at[0]).wait()
        if SPLIT[t] == 2:
            recv(full_part(t, me4, y, 1 - c)[1], init_sem.at[0], sib)
            relay_part(t, 0, 0)
            recv(wbuf.at[t, gx, z, 1 - y], init_sem.at[1 + t], ysame)
        else:
            recv(wbuf.at[t, gx, z], init_sem.at[1 + t], ysame)
        if t not in LATE:
            send(S_XMATE, mates(t, gx), mates(t, gx), mate_sem.at[t // 2], twin)

    def relay_part(t, d, k):
        for way, (zz, has, back, has_on, on) in enumerate((
                (z - d, z >= d, zm, has_zp, zp), (z + d, z + d < nz, zp, has_zm, zm))):
            ref = parts(t, zz, gx)[k]
            if d > 0:
                recv(ref, z_at(t, way, d, k), back, has)
            if d + 1 < nz:
                send(S_Z + 2 * d + way, ref, ref, z_at(t, way, d + 1, k), on, has & has_on if d > 0 else has_on)
            if d > 0:
                send(S_X, ref, ref, xsem.at[t // 2], twin, has)

    def relay(t, d):
        for k in range(SPLIT[t]):
            if d > 0 or k > 0 or SPLIT[t] != 2:
                relay_part(t, d, k)

    def finish(pair):
        if 2 * pair in LATE:
            recv(wbuf.at[2 * pair:2 * pair + 2, 1 - gx, z, 1 - y], late_sem, ysame)
        else:
            recv(wbuf.at[2 * pair:2 * pair + 2, 1 - gx, z, 1 - y], mate_sem.at[pair], twin)
        recv(wbuf.at[2 * pair:2 * pair + 2, 1 - gx, 0:nz - 1], xsem.at[pair], twin)

    def normalize(slot, first=0, count=None):
        step = 16
        count = rows if count is None else count

        def body(i, _):
            r = pl.ds(pl.multiple_of(first + i * step, step), step)
            wide = xraw[slot, r, :].astype(jnp.float32)
            inv = lax.rsqrt(jnp.mean(wide * wide, axis=-1, keepdims=True) + 1e-05)
            xn[slot, r, :] = (wide * inv * gain[...]).astype(jnp.bfloat16)
            return 0

        lax.fori_loop(0, count // step, body, 0)

    def tokens(j):
        r = slice(*pcuts[j:j + 2])
        recv(xraw.at[ys4, r], tok_sem.at[0, j], ysame)
        send(S_TOK, xraw.at[ys4, r], xraw.at[ys4, r], tok_sem.at[1, j], sib)
        normalize(ys4, r.start, r.stop - r.start)
        recv(xraw.at[yo4, r], tok_sem.at[1, j], sib)
        normalize(yo4, r.start, r.stop - r.start)

    def product(t, a):
        w = jnp.concatenate(
            [jnp.concatenate([wbuf[2 * t + i, h, zz, yc // 2, yc % 2] for i in range(2)], axis=1)
             for zz in range(nz) for yc in range(4) for h in range(2)], axis=0)
        return jnp.dot(a, w, preferred_element_type=jnp.float32).astype(jnp.bfloat16)

    def project(yy, lo, hi):
        n = hi - lo
        r = product(0, xn[pl.ds(2 * yy, 2), lo:hi, :].reshape(2 * n, width))
        for i in range(2):
            win[REACH + 2 * yy + i, lo:hi, :] = r[i * n:(i + 1) * n]

    def queries2(t, yy):
        r = product(t, xn[pl.ds(2 * yy, 2)].reshape(2 * rows, width))
        for i in range(2):
            for qb in range(NCH):
                for h in range(2):
                    lo = i * rows + qb * HD
                    qbuf[t - 1, 2 * yy + i, qb, h] = r[lo:lo + HD, h * HD:(h + 1) * HD]

    def halo_send(yy, lo, hi):
        r = slice(lo, hi)
        for slot in range(4):
            mine = (slot // 2) == yy
            a = win.at[REACH + slot, r]
            if slot > 0:
                send(S_UP, a, win.at[slot - 1, r], halo_sem.at[0], zp, mine & has_zp)
            if slot < 3:
                send(S_DOWN, a, win.at[REACH + 4 + slot, r], halo_sem.at[1], zm, mine & has_zm)

    def halo_recv():
        recv(win.at[0:REACH], halo_sem.at[0], zm, has_zm)
        recv(win.at[REACH + 4:SLOTS], halo_sem.at[1], zp, has_zp)

    def ids_send():
        recv(idwin.at[0:3 * NCH], id_sem.at[0], sib)
        edge = NCH * REACH
        a = NCH * (REACH + 4)
        send(S_IDUP, idwin.at[a - edge:a], idwin.at[0:edge], id_sem.at[1], zp, has_zp)
        send(S_IDDOWN, idwin.at[edge:2 * edge], idwin.at[a:a + edge], id_sem.at[2], zm, has_zm)

    def ids_recv():
        edge = NCH * REACH
        a = NCH * (REACH + 4)
        recv(idwin.at[0:edge], id_sem.at[1], zm, has_zm)
        recv(idwin.at[a:a + edge], id_sem.at[2], zp, has_zp)
        lane = lax.broadcasted_iota(jnp.int32, (8, HD), 1)
        ids = jnp.zeros((8, HD), jnp.int32)
        for j in range(SLOTS * NCH):
            ids = jnp.where(lane == j, idwin[j], ids)
        for j in range(edge, a):
            opening = jnp.min(jnp.where(ids == idwin[j], lane, j))
            starts[j - edge] = jnp.maximum(opening, j - edge)

    rate = HD ** (-0.5) * math.log2(math.e)
    span = REACH * NCH + 1

    def attend(slot, t):
        kv = win.reshape(SLOTS * NCH, HD, SW)
        for qb in range(NCH):
            mine = idwin[NCH * (REACH + slot) + qb, 0:1, :]
            start = starts[NCH * slot + qb]
            bias = jnp.concatenate(
                [jnp.where(idwin[start + j, 0:1, :] == mine, 0.0, -1e30) for j in range(span)], axis=1)
            q = qbuf[t, slot, qb].reshape(2 * HD, HD)
            at = pl.ds(start, span)
            k = kv[at, :, 0:HD].reshape(span * HD, HD)
            v = jnp.concatenate([kv[at, :, HD:SW].reshape(span * HD, HD),
                                 jnp.ones((span * HD, HD), jnp.bfloat16)], axis=1)
            sc = lax.dot_general(q, k, (((1,), (1,)), ((), ())), preferred_element_type=jnp.float32) + bias
            top = jnp.max(sc, axis=-1, keepdims=True)
            w = jnp.exp2((sc - top) * rate).astype(jnp.bfloat16)
            o = jnp.dot(w, v, preferred_element_type=jnp.float32)
            o = (o[:, 0:HD] / o[:, HD:SW]).astype(jnp.bfloat16)
            rr = slice(qb * HD, (qb + 1) * HD)
            obuf[t, slot, rr, 0:HD] = o[0:HD]
            obuf[t, slot, rr, HD:SW] = o[HD:SW]

    def out_cols(head, t):
        return out_ref.at[:, pl.ds(pl.multiple_of(head * (GQ * HD) + t * SW, HD), SW)]

    def start_local(src, dst):
        local(src, dst, 2)

    def attend_slot(t, slot):
        attend(slot, t)
        src = obuf.at[t, slot]
        pl.when(slot != me4)(lambda: send(S_OUT, src, out_cols(me4, t), out_sem, (g, 4 * z + slot)))
        pl.when(slot == me4)(lambda: start_local(src, out_cols(me4, t)))

    def over(first, stop, f):
        def body(i, _):
            f(2 * lax.rem(1 - y + i // 2, 2) + lax.rem(1 - c + i, 2))
            return 0

        lax.fori_loop(first, stop, body, 0)

    last = nz - 1
    held = ((5, last - 1), (4, last), (5, last))
    order = sorted(((t, d) for t in range(SETS) for d in range(nz) if (t, d) not in held),
                   key=lambda td: (nz - 1) * td[0] + (nz - 0.5) * td[1])
    after = {}

    def at_task(index, f):
        after.setdefault(min(index, len(order) - 1), []).append(f)

    def kv_early():
        finish(0)
        project(y, 0, rows)
        project(1 - y, 0, HD)
        halo_send(1 - y, 0, half)

    def kv_more():
        tokens(2)
        project(1 - y, half, quarter)
        halo_send(1 - y, half, quarter)
        halo_send(y, 0, rows)

    def own_tokens():
        loc_x.wait()
        loc_in[4].wait()
        normalize(me4)

    def sib_tokens():
        recv(xraw.at[sib4], tok_sem.at[2, 0], sib)
        normalize(sib4)
        pl.when(z < 1)(blank(0))
        pl.when(z + 1 >= nz)(blank(REACH + 4))

    at_task(order.index((2, 0)), own_tokens)
    at_task(order.index((3, 0)), ids_send)
    at_task(order.index((3, 0)), sib_tokens)
    at_task(order.index((0, last)), lambda: tokens(0))
    at_task(order.index((4, 1)), lambda: tokens(1))
    at_task(order.index((1, last)) + 2, kv_early)
    at_task(max(order.index((4, min(2, last))), order.index((1, last)) + 3), kv_more)
    gathered = moved = 0
    for i, (t, d) in enumerate(order):
        moved += d > 0
        while gathered < SETS and gathered <= max(t, moved + 1 if moved else 0):
            gather(gathered)
            gathered += 1
        relay(t, d)
        for f in after.get(i, ()):
            f()
    tokens(3)
    project(1 - y, quarter, eighth)
    halo_send(1 - y, quarter, eighth)
    tokens(4)
    tokens(5)
    project(1 - y, eighth, rows)
    halo_send(1 - y, eighth, rows)
    relay(*held[0])
    relay(*held[1])
    finish(1)
    queries2(1, 1 - y)
    queries2(1, y)
    ids_recv()
    halo_recv()
    over(0, 2, lambda slot: attend_slot(0, slot))
    relay(*held[2])

    def near(slot):
        attend_slot(0, slot)

    def late(slot):
        attend_slot(1, slot)

    over(2, 4, near)
    finish(2)
    queries2(2, 1 - y)
    over(0, 2, late)
    queries2(2, y)
    over(2, 4, late)
    recv(obuf.at[:, 0:3], out_sem, sib)
    pltpu.make_async_copy(obuf.at[:, 0], obuf.at[:, 0], loc_sem.at[2]).wait()
    sent(S_MATE, wbuf.at[:, 0, 0, 0])
    sent(S_LATE, wbuf.at[0:len(LATE), 0, 0, 0])
    sent(S_XMATE, wbuf.at[0:SETS - len(LATE), 0, 0, 0])
    sent(S_SIB, wbuf.at[:, :, 0, 0, 0])
    sent(S_IDS, idwin.at[0:3 * NCH])
    sent(S_IDUP, idwin.at[0:NCH * REACH], has_zp)
    sent(S_IDDOWN, idwin.at[0:NCH * REACH], has_zm)
    sent(S_TOK, xraw.at[0:3])
    sent(S_UP, win.at[0:REACH], has_zp)
    sent(S_DOWN, win.at[0:REACH], has_zm)
    sent(S_OUT, obuf.at[:, 0:3])
    sent(S_X, wbuf.at[:, 0, 0:nz - 1])
    for d in range(nz - 1):
        sent(S_Z + 2 * d, wbuf.at[:, 0, 0], has_zp & (z >= d))
        sent(S_Z + 2 * d + 1, wbuf.at[:, 0, 0], has_zm & (z + d < nz))


def solution(mesh):
    n_seq = mesh.shape["seq"]
    n_chips = n_seq // 2
    nz = n_chips // 2

    def on_device(tokens, norm_gain, w_query, w_key, w_value, passage_blocks):
        rows, width = tokens.shape
        anywhere = pl.BlockSpec(memory_space=pl.ANY)
        hbm = pl.BlockSpec(memory_space=pltpu.HBM)
        bf = jnp.bfloat16
        dma = pltpu.SemaphoreType.DMA
        half = w_query.shape[0] // 2
        halves = [w.reshape(2, half, w.shape[1]) for w in (w_query, w_key, w_value)]
        return pl.pallas_call(
            functools.partial(kernel, n_chips),
            out_shape=jax.ShapeDtypeStruct((rows, QH * HD), bf),
            in_specs=[hbm] * 6,
            out_specs=anywhere,
            scratch_shapes=[
                pltpu.VMEM((1, width), jnp.float32),
                pltpu.SMEM(passage_blocks.shape, jnp.int32),
                pltpu.SMEM((4 * NCH,), jnp.int32),
                pltpu.VMEM((4, rows, width), bf),
                pltpu.VMEM((4, rows, width), bf),
                *(pltpu.VMEM((2, half, w.shape[1]), bf) for w in (w_key, w_value, w_query)),
                pltpu.VMEM((SETS, 2, nz, 2, 2, half, HD), bf),
                pltpu.VMEM((2, 4, NCH, 2, HD, HD), bf),
                pltpu.VMEM((SLOTS, rows, SW), bf),
                pltpu.VMEM((SLOTS * NCH, 8, HD), jnp.int32),
                pltpu.VMEM((2, 4, rows, SW), bf),
                dma((S_Z + 2 * (nz - 1),)), dma((8,)), dma((1 + SETS,)), dma, dma((2,)),
                dma((sum(SPLIT) * sum(2 if 2 * d < nz else 1 for d in range(1, nz)),)), dma((3,)), dma((3, len(PIECES) - 1)), dma((3,)), dma((2,)), dma,
            ],
            compiler_params=pltpu.CompilerParams(
                collective_id=0, has_side_effects=True, vmem_limit_bytes=52 * 2**20),
        )(*(pltpu.with_memory_space_constraint(a, pltpu.HBM)
            for a in (tokens, norm_gain[None, :], *halves, passage_blocks)))

    in_specs = (
        P(("groups", "seq"), None),
        P(),
        P("seq", None),
        P("seq", None),
        P("seq", None),
        P(("groups", "seq")),
    )
    out_specs = P(("groups", "seq"), None)
    return jax.shard_map(on_device, mesh=mesh, in_specs=in_specs, out_specs=out_specs, check_vma=False)
```
